32 devices in a mesh: row: 8 (over y, x, core), col: 4 (over z).
Axes of the slice: x: 2, y: 2, z: 4, core: 2. Of those that a mesh axis runs over, the one named last changes fastest.
Arguments:
- embedding: bfloat16 [512, 256, 256], P('row', 'col'), may hold values from -6 to 6
- counts: int32 [4, 8], P('col'), may hold values from 1 to 48, 128 in all within a row
- points: int32 [8, 4, 2, 48], P('row', 'col'), may hold values from 0 to 1023
- pe_gauss: float32 [2, 128], replicated, may hold values from -6 to 6
- point_embed: float32 [256], replicated, may hold values from -6 to 6
- mask_token: float32 [256], replicated, may hold values from -6 to 6
- sa_qkv: bfloat16 [256, 768], replicated, may hold values from -0.375 to 0.375
- sa_out: bfloat16 [256, 256], replicated, may hold values from -0.375 to 0.375
- t2i_qkv: bfloat16 [256, 384], replicated, may hold values from -0.375 to 0.375
- t2i_out: bfloat16 [128, 256], replicated, may hold values from -0.5 to 0.5
- mlp_up: bfloat16 [256, 2048], replicated, may hold values from -0.375 to 0.375
- mlp_down: bfloat16 [2048, 256], replicated, may hold values from -0.125 to 0.125
- i2t_qkv: bfloat16 [256, 384], replicated, may hold values from -0.375 to 0.375
- i2t_out: bfloat16 [128, 256], replicated, may hold values from -0.5 to 0.5
- hyper_w: bfloat16 [2, 256, 256], replicated, may hold values from -0.375 to 0.375
- ln_gains: float32 [4, 256], replicated, may hold values from 0.1 to 1.9
Outputs:
- mask_logits: bfloat16 [8, 4, 48, 4096], P('row', 'col')
- seam_blend: float32 [512, 256], P('row', 'col')
The draws below stay inside these ranges and needn't reach their ends.
Inputs may be any that keep to these rules, and one draw needn't show every extreme that they name: For each column index the counts of its 8 tiles sum to 128, and the largest of them is 48. `points`: slots at or past a tile's count hold coordinates that no output reads.
All inputs are finite; a program needn't handle non-finite values.
Results may differ from the reference program's by a relative error of at most 0.012.
Values may be sent and summed in bfloat16 or wider, within the bound.
No kernel may reach another device: no remote copies, remote signals or barrier semaphores. Data moves between devices by JAX's collectives and lax.ppermute only.
A program may use at most 128 MiB of HBM per device.

```python
import math
import jax
import jax.numpy as jnp
import numpy as np
from jax import lax

D = 256
MLP = 2048
HEADS = 8
GRID = 64
SEAM = 4
DI = 128
IMG = 1024
CAP = 48
TOTAL = 128
N_ROW = 8
N_COL = 4


def place_ends(values, own_key, smallest, top_value):
    place = [jax.random.randint(jax.random.fold_in(own_key, axis), (), 0, length) for axis, length in enumerate(values.shape)]
    widest = values.shape.index(max(values.shape))
    next_to = place[:widest] + [(place[widest] + 1) % values.shape[widest]] + place[widest + 1:]
    return values.at[tuple(place)].set(smallest).at[tuple(next_to)].set(top_value)


def steps_of(stream_key, dims, cuts, smallest, largest):
    loudness = 1.0
    for position, parts in cuts:
        draws = jax.random.uniform(jax.random.fold_in(jax.random.fold_in(stream_key, 6), position), (parts,), jnp.float32, smallest / len(cuts), largest / len(cuts))
        loudness = loudness * jnp.repeat(jnp.exp(draws), dims[position] // parts).reshape((-1,) + (1,) * (len(dims) - 1 - position))
    return loudness


def profile(count, total, reach, skew):
    loads = [(1 << 20) // math.isqrt(standing ** skew) + 1 for standing in range(2, count + 1)]
    rest, given = total - reach - (count - 1), [1] * (count - 1)
    while rest > 0:
        candidates = [i for i in range(count - 1) if given[i] < reach]
        pool, budget = sum([loads[i] for i in candidates]), rest
        for i in candidates:
            addition = min(reach - given[i], max(1, budget * loads[i] // pool), rest)
            given[i] = given[i] + addition
            rest = rest - addition
    return np.array([reach] + given)


def ragged_sizes(own_key, amount, total, most, skew):
    if amount == 2:
        one = jax.random.randint(own_key, (), max(1, total - most), min(most, total - 1) + 1)
        return jnp.stack([one, total - one])
    tallies = jnp.asarray(profile(amount, total, most, skew), jnp.int32)
    twos = (amount - 1) // 2
    giver, sink = tallies[1:1 + 2 * twos:2], tallies[2:2 + 2 * twos:2]
    margin = jnp.minimum(giver - 1, most - sink)
    passed = jax.random.randint(jax.random.fold_in(own_key, 1), (twos,), 0, 1 << 20) % (margin + 1)
    tallies = tallies.at[1:1 + 2 * twos:2].set(giver - passed).at[2:2 + 2 * twos:2].set(sink + passed)
    return tallies[jax.random.permutation(jax.random.fold_in(own_key, 2), amount)]


def noise(own_key, shape, scale, reach, shards=(), kind=jnp.bfloat16):
    drawn = jax.random.normal(own_key, shape, jnp.float32) * scale
    if len(shards) > 0:
        drawn = steps_of(own_key, shape, shards, -0.22, 0.18) * drawn
    return jnp.clip(drawn, min=-reach, max=reach).astype(kind)


def setup_inputs(seed: int = 0) -> dict:
    splits = jax.random.split(jax.random.key(seed), 17)
    embedding = noise(splits[0], (N_ROW * GRID, N_COL * GRID, D), 1.0, 6.0, ((0, 8), (1, 4)))
    counts = jax.vmap(lambda own: ragged_sizes(own, N_ROW, TOTAL, CAP, 2))(jax.random.split(splits[1], N_COL)).reshape((N_COL, N_ROW)).astype(jnp.int32)
    points = place_ends(jax.random.randint(splits[2], (N_ROW, N_COL, 2, CAP), 0, IMG), jax.random.fold_in(splits[2], 1), 0, IMG - 1).astype(jnp.int32)
    pe_gauss = noise(splits[3], (2, D // 2), 1.0, 6.0, (), jnp.float32)
    point_embed = noise(splits[4], (D,), 1.0, 6.0, (), jnp.float32)
    mask_token = noise(splits[5], (D,), 1.0, 6.0, (), jnp.float32)
    sa_qkv = noise(splits[6], (D, 3 * D), D ** -0.5, 0.375)
    sa_out = noise(splits[7], (D, D), D ** -0.5, 0.375)
    t2i_qkv = noise(splits[8], (D, 3 * DI), D ** -0.5, 0.375)
    t2i_out = noise(splits[9], (DI, D), DI ** -0.5, 0.5)
    mlp_up = noise(splits[10], (D, MLP), D ** -0.5, 0.375)
    mlp_down = noise(splits[11], (MLP, D), MLP ** -0.5, 0.125)
    i2t_qkv = noise(splits[12], (D, 3 * DI), D ** -0.5, 0.375)
    i2t_out = noise(splits[13], (DI, D), DI ** -0.5, 0.5)
    hyper_w = noise(splits[14], (2, D, D), D ** -0.5, 0.375)
    ln_gains = jnp.clip(1.0 + 0.18 * jax.random.normal(splits[15], (4, D), jnp.float32), 0.1, 1.9)
    return dict(embedding=embedding, counts=counts, points=points, pe_gauss=pe_gauss, point_embed=point_embed, mask_token=mask_token, sa_qkv=sa_qkv, sa_out=sa_out, t2i_qkv=t2i_qkv, t2i_out=t2i_out, mlp_up=mlp_up, mlp_down=mlp_down, i2t_qkv=i2t_qkv, i2t_out=i2t_out, hyper_w=hyper_w, ln_gains=ln_gains)


norm_eps = 1e-05
highest = lax.Precision.HIGHEST

def layer_norm(values, norm_gain):
    row_mean = lax.optimization_barrier(jnp.mean(values, axis=-1, keepdims=True))
    centred = values - row_mean
    row_var = lax.optimization_barrier(jnp.mean(centred * centred, axis=-1, keepdims=True))
    return centred * lax.rsqrt(row_var + norm_eps) * norm_gain

def weight_dot(values, weight):
    return jnp.dot(values, weight.astype(jnp.float32), precision=highest)

def fourier(norm_x, norm_y, pe_gauss):
    phases = 2.0 * math.pi * ((2.0 * norm_x - 1.0)[:, None] * pe_gauss[0] + (2.0 * norm_y - 1.0)[:, None] * pe_gauss[1])
    return jnp.concatenate([jnp.sin(phases), jnp.cos(phases)], axis=-1)

def dense_pe(pixel_ids, grid_side, pe_gauss):
    norm_x = ((pixel_ids % grid_side).astype(jnp.float32) + 0.5) / grid_side
    norm_y = ((pixel_ids // grid_side).astype(jnp.float32) + 0.5) / grid_side
    return fourier(norm_x, norm_y, pe_gauss)

def softmax_last(scores):
    row_top = lax.optimization_barrier(jnp.max(scores, axis=-1, keepdims=True))
    exp_scores = jnp.exp(scores - row_top)
    return exp_scores / lax.optimization_barrier(jnp.sum(exp_scores, axis=-1, keepdims=True))

def token_side(points_xy, keys_pe, tile_flat, pe_gauss, point_embed, mask_token, sa_qkv, sa_out, t2i_qkv, t2i_out, mlp_up, mlp_down, i2t_qkv, hyper_w, ln_gains):
    slot_count = points_xy.shape[1]
    model_width = keys_pe.shape[1]
    pixel_count = keys_pe.shape[0]
    inner_width = t2i_qkv.shape[1] // 3
    self_width = model_width // HEADS
    head_width = inner_width // HEADS
    coords = (points_xy.astype(jnp.float32) + 0.5) / IMG
    prompt = fourier(coords[0], coords[1], pe_gauss) + point_embed
    start_tok = jnp.stack([jnp.broadcast_to(mask_token, (slot_count, model_width)), prompt], axis=1)
    self_qkv = weight_dot(start_tok, sa_qkv).reshape(slot_count, 2, 3, HEADS, self_width)
    self_score = jnp.einsum('cqhd,ckhd->chqk', self_qkv[:, :, 0], self_qkv[:, :, 1], precision=highest) / math.sqrt(self_width)
    self_out = jnp.einsum('chqk,ckhd->cqhd', softmax_last(self_score), self_qkv[:, :, 2], precision=highest)
    queries = layer_norm(weight_dot(self_out.reshape(slot_count, 2, model_width), sa_out), ln_gains[0])
    cross_q = weight_dot(queries + start_tok, t2i_qkv[:, :inner_width]).astype(jnp.bfloat16)
    cross_k = jnp.dot(keys_pe, t2i_qkv[:, inner_width:2 * inner_width], preferred_element_type=jnp.float32).astype(jnp.bfloat16)
    cross_v = jnp.dot(tile_flat, t2i_qkv[:, 2 * inner_width:], preferred_element_type=jnp.float32).astype(jnp.bfloat16)
    cross_score = jnp.einsum('cqhd,phd->chqp', cross_q.reshape(slot_count, 2, HEADS, head_width).astype(jnp.float32), cross_k.reshape(pixel_count, HEADS, head_width).astype(jnp.float32), precision=highest) / math.sqrt(head_width)
    cross_prob = softmax_last(cross_score).astype(jnp.bfloat16)
    cross_out = jnp.einsum('chqp,phd->cqhd', cross_prob.astype(jnp.float32), cross_v.reshape(pixel_count, HEADS, head_width).astype(jnp.float32), precision=highest)
    queries = layer_norm(queries + weight_dot(cross_out.reshape(slot_count, 2, inner_width), t2i_out), ln_gains[1])
    hidden = jax.nn.relu(weight_dot(queries, mlp_up))
    queries = layer_norm(queries + weight_dot(hidden, mlp_down), ln_gains[2])
    back_k = weight_dot(queries + start_tok, i2t_qkv[:, inner_width:2 * inner_width]).astype(jnp.bfloat16)
    back_v = weight_dot(queries, i2t_qkv[:, 2 * inner_width:]).astype(jnp.bfloat16)
    kv_rows = jnp.concatenate([back_k, back_v], axis=1)
    hyper_rows = weight_dot(jax.nn.relu(weight_dot(queries[:, 0], hyper_w[0])), hyper_w[1]).astype(jnp.bfloat16)
    return (kv_rows, hyper_rows)

def image_side(tile_rows, query_rows, kv_rows, hyper_rows, out_weight, norm_gain):
    batch_rows, pix_rows, inner_width = query_rows.shape
    head_width = inner_width // HEADS
    head_query = query_rows.reshape(batch_rows, pix_rows, HEADS, head_width).astype(jnp.float32)
    head_keys = kv_rows[:, 0:2].reshape(batch_rows, 2, HEADS, head_width).astype(jnp.float32)
    values = kv_rows[:, 2:4].reshape(batch_rows, 2, HEADS, head_width).astype(jnp.float32)
    scores = jnp.einsum('bphd,bkhd->bphk', head_query, head_keys, precision=highest) / math.sqrt(head_width)
    attention = softmax_last(scores)
    mixture = jnp.einsum('bphk,bkhd->bphd', attention, values, precision=highest)
    mixture = mixture.reshape(batch_rows, pix_rows, inner_width).astype(jnp.bfloat16)
    update = jnp.einsum('bpi,id->bpd', mixture.astype(jnp.float32), out_weight.astype(jnp.float32), precision=highest)
    normed = layer_norm(tile_rows.astype(jnp.float32) + update, norm_gain)
    model_width = normed.shape[-1]
    return (lax.optimization_barrier(jnp.sum(normed * hyper_rows.astype(jnp.float32)[:, None, :], axis=-1)) / math.sqrt(model_width)).astype(jnp.bfloat16)

def reference(embedding, counts, points, pe_gauss, point_embed, mask_token, sa_qkv, sa_out, t2i_qkv, t2i_out, mlp_up, mlp_down, i2t_qkv, i2t_out, hyper_w, ln_gains):
    grid_side = GRID
    pixel_count = grid_side * grid_side
    row_count = N_ROW
    col_count = N_COL
    tile_total = row_count * col_count
    tiles = embedding.reshape(row_count, grid_side, col_count, grid_side, D).transpose(0, 2, 1, 3, 4).reshape(tile_total, pixel_count, D)
    tile_points = points.reshape(tile_total, 2, CAP)
    image_pe = dense_pe(jnp.arange(pixel_count, dtype=jnp.int32), grid_side, pe_gauss)

    def per_tile(tile_item):
        tile_flat, points_xy = tile_item
        keys_pe = (tile_flat.astype(jnp.float32) + image_pe).astype(jnp.bfloat16)
        kv_rows, hyper_rows = token_side(points_xy, keys_pe, tile_flat, pe_gauss, point_embed, mask_token, sa_qkv, sa_out, t2i_qkv, t2i_out, mlp_up, mlp_down, i2t_qkv, hyper_w, ln_gains)
        image_query = jnp.dot(keys_pe, i2t_qkv[:, :DI], preferred_element_type=jnp.float32).astype(jnp.bfloat16)
        return (kv_rows, hyper_rows, image_query)
    kv_all, hyper_all, query_all = lax.map(per_tile, (tiles, tile_points))
    live_flat = counts.T.reshape(tile_total).astype(jnp.int32)
    count_ends = jnp.cumsum(live_flat).astype(jnp.int32)
    count_starts = (count_ends - live_flat).astype(jnp.int32)
    live_total = col_count * TOTAL
    packed_order = jnp.arange(live_total, dtype=jnp.int32)
    tile_of = lax.optimization_barrier(jnp.sum((packed_order[:, None] >= count_ends[None, :]).astype(jnp.int32), axis=1)).astype(jnp.int32)
    slot_of = (packed_order - count_starts[tile_of]).astype(jnp.int32)

    def per_block(packed_ids):
        tile_ids, slot_ids = packed_ids
        return image_side(tiles[tile_ids], query_all[tile_ids], kv_all[tile_ids, slot_ids], hyper_all[tile_ids, slot_ids], i2t_out, ln_gains[3])
    logits = lax.map(per_block, (tile_of.reshape(-1, row_count), slot_of.reshape(-1, row_count))).reshape(live_total, pixel_count)
    mask_logits = jnp.zeros((tile_total, CAP, pixel_count), jnp.bfloat16).at[tile_of, slot_of].set(logits)
    keep_slot = jnp.arange(CAP, dtype=jnp.int32)[None, :, None] < live_flat[:, None, None]
    coverage = lax.optimization_barrier(jnp.sum(jnp.where(keep_slot, jax.nn.sigmoid(mask_logits.astype(jnp.float32)), jnp.float32(0.0)), axis=1))
    coverage = coverage.reshape(row_count, col_count, grid_side, grid_side).transpose(0, 2, 1, 3).reshape(row_count * grid_side, col_count * grid_side)
    padded = jnp.pad(coverage, ((0, 0), (SEAM, SEAM)))
    width_all = col_count * grid_side
    blended = jnp.zeros_like(coverage)
    for offset in range(-SEAM, SEAM + 1):
        factor = (SEAM + 1 - abs(offset)) / (SEAM + 1) ** 2
        blended = blended + factor * padded[:, SEAM + offset:SEAM + offset + width_all]
    return (mask_logits.reshape(row_count, col_count, CAP, pixel_count), blended)
```

```python
import functools
import math

import jax
import jax.numpy as jnp
from jax import lax
from jax.experimental import pallas as pl
from jax.experimental.pallas import tpu as pltpu
from jax.sharding import PartitionSpec as P

HEADS = 8
SEAM = 4
IMG = 1024
ROWS_AT_ONCE = 384
CELLS_AT_ONCE = 512

norm_eps = 1e-05
bf16 = jnp.bfloat16
f32 = jnp.float32


def mm(left, right):
    return lax.dot_general(left, right, (((1,), (0,)), ((), ())), preferred_element_type=f32)


def mm_t(left, right):
    return lax.dot_general(left, right, (((1,), (1,)), ((), ())), preferred_element_type=f32)


def halves(values):
    high = values.astype(bf16)
    low = (values - high.astype(f32)).astype(bf16)
    return jnp.concatenate([high, low], axis=0)


def wide_mm(values, weight, product=mm):
    rows = values.shape[0]
    both = product(halves(values), weight)
    return both[:rows] + both[rows:]


def layer_norm(values, gain):
    centred = values - jnp.mean(values, axis=-1, keepdims=True)
    spread = jnp.mean(centred * centred, axis=-1, keepdims=True)
    return centred * lax.rsqrt(spread + norm_eps) * gain


def sin_turns(turns):
    part = turns - jnp.floor(turns + 0.5)
    size = 0.25 - jnp.abs(jnp.abs(part) - 0.25)
    angle = (2.0 * math.pi) * jnp.where(part < 0.0, -size, size)
    square = angle * angle
    total = jnp.full_like(angle, -1.0 / math.factorial(11))
    for order in (9, 7, 5, 3, 1):
        sign = 1.0 if order % 4 == 1 else -1.0
        total = total * square + sign / math.factorial(order)
    return total * angle


def by_head(rows, inner_width):
    head_width = inner_width // HEADS
    lane = lax.broadcasted_iota(jnp.int32, rows.shape, 1)
    return jnp.concatenate(
        [
            jnp.where((lane >= h * head_width) & (lane < (h + 1) * head_width), rows, 0.0)
            for h in range(HEADS)
        ],
        axis=0,
    )


def group_ones(width, group):
    row = lax.broadcasted_iota(jnp.int32, (width, width), 0)
    column = lax.broadcasted_iota(jnp.int32, (width, width), 1)
    first = row - lax.rem(row, group)
    return jnp.where((column >= first) & (column < first + group), 1.0, 0.0).astype(bf16)


def decode_kernel(
    counts_ref,
    points_ref,
    gauss_ref,
    point_embed_ref,
    mask_token_ref,
    sa_qkv_ref,
    sa_out_ref,
    t2i_qkv_ref,
    t2i_out_ref,
    mlp_up_ref,
    mlp_down_ref,
    i2t_qkv_ref,
    i2t_out_ref,
    hyper_ref,
    gains_ref,
    cells_ref,
    logits_ref,
    coverage_ref,
    keys_ref,
    table_ref,
    pooled_ref,
):
    pixels, width = cells_ref.shape
    side = math.isqrt(pixels)
    slots = points_ref.shape[1]
    inner = t2i_qkv_ref.shape[1] // 3
    half = width // 2
    live = counts_ref[0, lax.axis_index("row")]

    gauss = gauss_ref[...]
    steps = lax.broadcasted_iota(jnp.int32, (side, half), 0).astype(f32)
    steps = (2.0 * (steps + 0.5)) / side - 1.0
    spots = jnp.clip(points_ref[...], 0, IMG - 1).astype(f32)
    spots = 2.0 * ((spots + 0.5) / IMG) - 1.0
    same = lax.broadcasted_iota(jnp.int32, (slots, slots), 0) == lax.broadcasted_iota(
        jnp.int32, (slots, slots), 1
    )
    spot_x = jnp.sum(jnp.where(same, spots[0:1], 0.0), axis=1, keepdims=True)
    spot_y = jnp.sum(jnp.where(same, spots[1:2], 0.0), axis=1, keepdims=True)
    turns = jnp.concatenate(
        [steps * gauss[0:1], steps * gauss[1:2], spot_x * gauss[0:1] + spot_y * gauss[1:2]], axis=0
    )
    sines = sin_turns(turns)
    cosines = sin_turns(turns + 0.25)
    prompt = jnp.concatenate([sines[2 * side :], cosines[2 * side :]], axis=1)
    table_ref[0] = sines[: 2 * side]
    table_ref[1] = cosines[: 2 * side]

    sin_x, cos_x = sines[:side], cosines[:side]

    def one_line(line, carry):
        sin_y = table_ref[0, pl.ds(side + line, 1), :]
        cos_y = table_ref[1, pl.ds(side + line, 1), :]
        place = pl.ds(pl.multiple_of(line * side, side), side)
        encoding = jnp.concatenate(
            [sin_x * cos_y + cos_x * sin_y, cos_x * cos_y - sin_x * sin_y], axis=1
        )
        keys_ref[place, :] = (cells_ref[place, :].astype(f32) + encoding).astype(bf16)
        return carry

    lax.fori_loop(0, side, one_line, 0, unroll=4)

    start = jnp.concatenate(
        [
            jnp.broadcast_to(mask_token_ref[...], (slots, width)),
            prompt + point_embed_ref[...],
        ],
        axis=0,
    )
    qkv = wide_mm(start, sa_qkv_ref[...])
    query, key, value = qkv[:, :width], qkv[:, width : 2 * width], qkv[:, 2 * width :]
    key_gap = key[:slots] - key[slots:]
    value_gap = value[:slots] - value[slots:]
    scores = wide_mm(
        query * jnp.concatenate([key_gap, key_gap], axis=0), group_ones(width, width // HEADS)
    )
    first = 0.5 * jnp.tanh((0.5 / math.sqrt(width // HEADS)) * scores) + 0.5
    attended = jnp.concatenate([value[slots:]] * 2, axis=0) + first * jnp.concatenate(
        [value_gap, value_gap], axis=0
    )
    queries = layer_norm(wide_mm(attended, sa_out_ref[...]), gains_ref[0:1])

    head_scale = 1.0 / math.sqrt(inner // HEADS)
    cross_q = wide_mm(queries + start, t2i_qkv_ref[:, :inner])
    cross_q = by_head(cross_q, inner).astype(bf16)
    probes = mm_t(cross_q, t2i_qkv_ref[:, inner : 2 * inner]) * (head_scale * math.log2(math.e))
    probes = probes.astype(bf16)
    probe_rows = probes.shape[0]
    for at in range(0, probe_rows, ROWS_AT_ONCE):
        raw = mm_t(probes[at : at + ROWS_AT_ONCE], keys_ref[...])
        raw = jnp.exp2(raw - jnp.max(raw, axis=1, keepdims=True))
        total = jnp.sum(raw, axis=1, keepdims=True)
        pooled_ref[at : at + ROWS_AT_ONCE, :] = mm(raw.astype(bf16), cells_ref[...]) / total
    pooled = wide_mm(pooled_ref[...], t2i_qkv_ref[:, 2 * inner :])
    tokens = start.shape[0]
    lane = lax.broadcasted_iota(jnp.int32, (tokens, inner), 1)
    head_width = inner // HEADS
    joined = jnp.zeros((tokens, inner), f32)
    for h in range(HEADS):
        own = (lane >= h * head_width) & (lane < (h + 1) * head_width)
        joined = joined + jnp.where(own, pooled[h * tokens : (h + 1) * tokens], 0.0)
    queries = layer_norm(queries + wide_mm(joined, t2i_out_ref[...]), gains_ref[1:2])
    hidden = jnp.maximum(wide_mm(queries, mlp_up_ref[...]), 0.0)
    queries = layer_norm(queries + wide_mm(hidden, mlp_down_ref[...]), gains_ref[2:3])

    back_k = wide_mm(queries + start, i2t_qkv_ref[:, inner : 2 * inner])
    back_v = wide_mm(queries, i2t_qkv_ref[:, 2 * inner :])
    gaps = by_head(back_k[:slots] - back_k[slots:], inner)
    gaps = wide_mm(gaps, i2t_qkv_ref[:, :inner], mm_t) * (0.5 * head_scale)
    gaps = gaps.astype(bf16)
    middle = 0.5 * (back_v[:slots] + back_v[slots:])
    apart = by_head(0.5 * (back_v[:slots] - back_v[slots:]), inner)
    moves = wide_mm(jnp.concatenate([apart, middle], axis=0), i2t_out_ref[...])
    moves = (moves - jnp.mean(moves, axis=1, keepdims=True)).astype(bf16)
    hyper = wide_mm(jnp.maximum(wide_mm(queries[:slots], hyper_ref[0]), 0.0), hyper_ref[1])
    hyper = hyper.astype(bf16).astype(f32) * gains_ref[3:4]
    hyper = (hyper - jnp.mean(hyper, axis=1, keepdims=True)).astype(bf16)
    spread = HEADS * slots
    apart, middle = moves[:spread], moves[spread:]
    middle_wide, hyper_wide = middle.astype(f32), hyper.astype(f32)
    middle_norm = jnp.sum(middle_wide * middle_wide, axis=1, keepdims=True)
    middle_mask = jnp.sum(middle_wide * hyper_wide, axis=1, keepdims=True)
    doubled = (2.0 * moves.astype(f32)).astype(bf16)
    on_cells = jnp.concatenate([doubled, hyper], axis=0)
    on_weights = mm_t(jnp.concatenate([apart, doubled[spread:], hyper], axis=0), apart)
    row_slot = lax.rem(lax.broadcasted_iota(jnp.int32, on_weights.shape, 0), slots)
    column_slot = lax.rem(lax.broadcasted_iota(jnp.int32, on_weights.shape, 1), slots)
    on_weights = jnp.where(row_slot == column_slot, on_weights, 0.0).astype(bf16)

    row = lax.broadcasted_iota(jnp.int32, (width, width), 0)
    column = lax.broadcasted_iota(jnp.int32, (width, width), 1)
    centring = jnp.where(row == column, 1.0 - 1.0 / width, -1.0 / width).astype(bf16)
    ones = jnp.ones((8, width), bf16)
    kept = lax.broadcasted_iota(jnp.int32, (slots, CELLS_AT_ONCE), 0) < live

    def some_cells(index, carry):
        place = pl.ds(pl.multiple_of(index * CELLS_AT_ONCE, CELLS_AT_ONCE), CELLS_AT_ONCE)
        cells = cells_ref[place, :]
        weights = jnp.tanh(mm_t(gaps, keys_ref[place, :]))
        centred = mm(cells, centring)
        squares = halves(centred * centred)
        norms = mm_t(ones, squares)
        norms = norms[:, :CELLS_AT_ONCE] + norms[:, CELLS_AT_ONCE:]
        both = mm_t(on_cells, cells) + mm(on_weights, weights.astype(bf16))
        square = both[spread : spread + slots] + middle_norm
        square = square + jnp.concatenate([norms] * (slots // 8), axis=0)
        for h in range(HEADS):
            part = slice(h * slots, (h + 1) * slots)
            square = square + weights[part] * both[part]
        dots = both[spread + slots :] + middle_mask
        logits = dots * lax.rsqrt(jnp.maximum(square, 0.0) + width * norm_eps)
        logits = jnp.where(kept, logits, 0.0).astype(bf16)
        logits_ref[:, place] = logits
        shares = jnp.where(kept, 0.5 * jnp.tanh(0.5 * logits.astype(f32)) + 0.5, 0.0)
        shares = jnp.sum(shares, axis=0, keepdims=True)
        lines = CELLS_AT_ONCE // 128
        for line in range(lines):
            coverage_ref[pl.ds(index * lines + line, 1), :] = shares[
                :, line * 128 : (line + 1) * 128
            ]
        return carry

    lax.fori_loop(0, pixels // CELLS_AT_ONCE, some_cells, 0)


def padded_2(cells, sides, width):
    for axis, dim in sides:
        count = lax.axis_size(axis)
        ends = count - 1
        head = lax.slice_in_dim(cells, 0, width, axis=dim)
        tail = lax.slice_in_dim(cells, cells.shape[dim] - width, cells.shape[dim], axis=dim)
        cells = jnp.concatenate(
            [
                lax.ppermute(tail, axis, [(i, (i + 1) % count) for i in range(ends)]),
                cells,
                lax.ppermute(head, axis, [((i + 1) % count, i) for i in range(ends)]),
            ],
            axis=dim,
        )
    return cells


def shards(
    embedding,
    counts,
    points,
    pe_gauss,
    point_embed,
    mask_token,
    sa_qkv,
    sa_out,
    t2i_qkv,
    t2i_out,
    mlp_up,
    mlp_down,
    i2t_qkv,
    i2t_out,
    hyper_w,
    ln_gains,
):
    side = embedding.shape[0]
    width = embedding.shape[2]
    inner = t2i_qkv.shape[1] // 3
    slots = points.shape[3]
    pixels = side * side
    whole = pl.BlockSpec(memory_space=pltpu.VMEM)
    logits, coverage = pl.pallas_call(
        decode_kernel,
        out_shape=(
            jax.ShapeDtypeStruct((slots, pixels), bf16),
            jax.ShapeDtypeStruct((pixels // 128, 128), f32),
        ),
        in_specs=[pl.BlockSpec(memory_space=pltpu.SMEM)] + [whole] * 15,
        out_specs=(whole, whole),
        scratch_shapes=[
            pltpu.VMEM((pixels, width), bf16),
            pltpu.VMEM((2, 2 * side, width // 2), f32),
            pltpu.VMEM((2 * slots * HEADS, width), f32),
        ],
        compiler_params=pltpu.CompilerParams(vmem_limit_bytes=58 << 20),
        name="decode",
    )(
        counts,
        points.reshape(2, slots),
        pe_gauss,
        point_embed.reshape(1, width),
        mask_token.reshape(1, width),
        sa_qkv,
        sa_out,
        t2i_qkv,
        t2i_out,
        mlp_up,
        mlp_down,
        i2t_qkv,
        i2t_out,
        hyper_w,
        ln_gains,
        embedding.reshape(pixels, width),
    )
    coverage = coverage.reshape(side, side)
    padded = padded_2(coverage, (("col", 1),), SEAM)
    blended = jnp.zeros_like(coverage)
    for offset in range(-SEAM, SEAM + 1):
        factor = (SEAM + 1 - abs(offset)) / (SEAM + 1) ** 2
        blended = blended + factor * padded[:, SEAM + offset : SEAM + offset + side]
    return (logits.reshape(1, 1, slots, pixels), blended)


def solution(mesh):
    placed = (P("row", "col", None), P("col", None), P("row", "col", None, None)) + (P(),) * 13
    return jax.shard_map(
        shards,
        mesh=mesh,
        in_specs=placed,
        out_specs=(P("row", "col", None, None), P("row", "col")),
        check_vma=False,
    )
```

```python
import functools
import math

import jax
import jax.numpy as jnp
from jax import lax
from jax.experimental import pallas as pl
from jax.experimental.pallas import tpu as pltpu
from jax.sharding import PartitionSpec as P

HEADS = 8
SEAM = 4
IMG = 1024
SLOT_GROUP = 16
KEYS_AT_ONCE = 1024
PROBES_AT_ONCE = 256
CELLS_AT_ONCE = 512

norm_eps = 1e-05
bf16 = jnp.bfloat16
f32 = jnp.float32


def mm(left, right):
    return lax.dot_general(left, right, (((1,), (0,)), ((), ())), preferred_element_type=f32)


def mm_t(left, right):
    return lax.dot_general(left, right, (((1,), (1,)), ((), ())), preferred_element_type=f32)


def halves(values):
    high = values.astype(bf16)
    low = (values - high.astype(f32)).astype(bf16)
    return jnp.concatenate([high, low], axis=0)


def wide_mm(values, weight, product=mm):
    rows = values.shape[0]
    both = product(halves(values), weight)
    return both[:rows] + both[rows:]


def layer_norm(values, gain):
    centred = values - jnp.mean(values, axis=-1, keepdims=True)
    spread = jnp.mean(centred * centred, axis=-1, keepdims=True)
    return centred * lax.rsqrt(spread + norm_eps) * gain


def sin_turns(turns):
    part = turns - jnp.floor(turns + 0.5)
    size = 0.25 - jnp.abs(jnp.abs(part) - 0.25)
    angle = (2.0 * math.pi) * jnp.where(part < 0.0, -size, size)
    square = angle * angle
    total = jnp.full_like(angle, -1.0 / math.factorial(11))
    for order in (9, 7, 5, 3, 1):
        sign = 1.0 if order % 4 == 1 else -1.0
        total = total * square + sign / math.factorial(order)
    return total * angle


def by_head(rows, inner_width):
    head_width = inner_width // HEADS
    lane = lax.broadcasted_iota(jnp.int32, rows.shape, 1)
    return jnp.concatenate(
        [
            jnp.where((lane >= h * head_width) & (lane < (h + 1) * head_width), rows, 0.0)
            for h in range(HEADS)
        ],
        axis=0,
    )


def by_group(rows, inner_width):
    return jnp.concatenate(
        [
            by_head(rows[at : at + SLOT_GROUP], inner_width)
            for at in range(0, rows.shape[0], SLOT_GROUP)
        ],
        axis=0,
    )


def group_ones(width, group):
    row = lax.broadcasted_iota(jnp.int32, (width, width), 0)
    column = lax.broadcasted_iota(jnp.int32, (width, width), 1)
    first = row - lax.rem(row, group)
    return jnp.where((column >= first) & (column < first + group), 1.0, 0.0).astype(bf16)


def cell_weights(gaps, keys):
    return jnp.tanh(mm_t(gaps, keys)).astype(bf16)


def cell_logits(weights, cells, on_cells, on_weights, consts, live):
    count, width = cells.shape
    slots = consts.shape[0]
    block = HEADS * SLOT_GROUP
    tall = block + 2 * SLOT_GROUP
    flat = mm_t(on_cells, cells)
    wide = cells.astype(f32)
    norms = mm_t(jnp.ones((SLOT_GROUP, width), bf16), halves(wide * wide))
    total = flat[slots // SLOT_GROUP * tall :][:SLOT_GROUP]
    norms = norms[:, :count] + norms[:, count:] - total * total * (1.0 / width)
    logits, covers = [], []
    for at in range(0, slots, SLOT_GROUP):
        group = at // SLOT_GROUP
        mine = weights[group * block : (group + 1) * block]
        both = flat[group * tall : (group + 1) * tall] + mm(
            on_weights[group * tall : (group + 1) * tall], mine
        )
        square = norms + both[block : block + SLOT_GROUP] + consts[at : at + SLOT_GROUP, 0:1]
        for h in range(HEADS):
            part = slice(h * SLOT_GROUP, (h + 1) * SLOT_GROUP)
            square = square + mine[part].astype(f32) * both[part]
        dots = both[block + SLOT_GROUP :] + consts[at : at + SLOT_GROUP, 1:2]
        kept = at + lax.broadcasted_iota(jnp.int32, (SLOT_GROUP, count), 0) < live
        found = dots * lax.rsqrt(jnp.maximum(square, 0.0) + width * norm_eps)
        found = jnp.where(kept, found, 0.0).astype(bf16)
        logits.append(found)
        covers.append(jnp.where(kept, 0.5 * jnp.tanh(0.5 * found.astype(f32)) + 0.5, 0.0))
    return jnp.concatenate(logits, axis=0), jnp.sum(sum(covers), axis=0, keepdims=True)


def decode_kernel(
    counts_ref,
    points_ref,
    gauss_ref,
    point_embed_ref,
    mask_token_ref,
    sa_qkv_ref,
    sa_out_ref,
    t2i_qkv_ref,
    t2i_out_ref,
    mlp_up_ref,
    mlp_down_ref,
    i2t_qkv_ref,
    i2t_out_ref,
    hyper_ref,
    gains_ref,
    cells_ref,
    keys_ref,
    gaps_ref,
    on_cells_ref,
    on_weights_ref,
    consts_ref,
    to_left_ref,
    to_right_ref,
    seam_cells_ref,
    seam_keys_ref,
    values_ref,
    pooled_ref,
):
    pixels, width = cells_ref.shape
    side = math.isqrt(pixels)
    slots = points_ref.shape[1]
    inner = t2i_qkv_ref.shape[1] // 3
    head_width = inner // HEADS
    half = width // 2
    live = counts_ref[0, lax.axis_index("row")]

    gauss = gauss_ref[...]
    steps = lax.broadcasted_iota(jnp.int32, (side, half), 0).astype(f32)
    steps = (2.0 * (steps + 0.5)) / side - 1.0
    spots = jnp.clip(points_ref[...], 0, IMG - 1).astype(f32)
    spots = 2.0 * ((spots + 0.5) / IMG) - 1.0
    same = lax.broadcasted_iota(jnp.int32, (slots, slots), 0) == lax.broadcasted_iota(
        jnp.int32, (slots, slots), 1
    )
    spot_x = jnp.sum(jnp.where(same, spots[0:1], 0.0), axis=1, keepdims=True)
    spot_y = jnp.sum(jnp.where(same, spots[1:2], 0.0), axis=1, keepdims=True)
    turns = jnp.concatenate(
        [steps * gauss[0:1], steps * gauss[1:2], spot_x * gauss[0:1] + spot_y * gauss[1:2]], axis=0
    )
    sines = sin_turns(turns)
    cosines = sin_turns(turns + 0.25)
    prompt = jnp.concatenate([sines[2 * side :], cosines[2 * side :]], axis=1)

    start = jnp.concatenate(
        [
            jnp.broadcast_to(mask_token_ref[...], (slots, width)),
            prompt + point_embed_ref[...],
        ],
        axis=0,
    )
    qkv = wide_mm(start, sa_qkv_ref[...])
    query, key, value = qkv[:, :width], qkv[:, width : 2 * width], qkv[:, 2 * width :]
    key_gap = key[:slots] - key[slots:]
    value_gap = value[:slots] - value[slots:]
    scores = wide_mm(
        query * jnp.concatenate([key_gap, key_gap], axis=0), group_ones(width, width // HEADS)
    )
    first = 0.5 * jnp.tanh((0.5 / math.sqrt(width // HEADS)) * scores) + 0.5
    attended = jnp.concatenate([value[slots:]] * 2, axis=0) + first * jnp.concatenate(
        [value_gap, value_gap], axis=0
    )
    queries = layer_norm(wide_mm(attended, sa_out_ref[...]), gains_ref[0:1])
    head_scale = 1.0 / math.sqrt(head_width)
    cross_q = wide_mm(queries + start, t2i_qkv_ref[:, :inner])
    cross_q = by_head(cross_q, inner).astype(bf16)
    probes = mm_t(cross_q, t2i_qkv_ref[:, inner : 2 * inner]) * (head_scale * math.log2(math.e))
    probes = probes.astype(bf16)

    sin_x, cos_x = sines[:side], cosines[:side]
    left_half = lax.broadcasted_iota(jnp.int32, (2 * SEAM, width), 0) < SEAM
    for line in range(side):
        sin_y, cos_y = sines[side + line : side + line + 1], cosines[side + line : side + line + 1]
        place = slice(line * side, (line + 1) * side)
        encoding = jnp.concatenate(
            [sin_x * cos_y + cos_x * sin_y, cos_x * cos_y - sin_x * sin_y], axis=1
        )
        own = cells_ref[place, :].astype(f32)
        keys = own + encoding
        keys_ref[place, :] = keys.astype(bf16)
        seam = slice(line * 2 * SEAM, (line + 1) * 2 * SEAM)
        seam_cells_ref[seam, :] = jnp.where(left_half, own[: 2 * SEAM], own[side - 2 * SEAM :])
        seam_keys_ref[seam, :] = jnp.where(left_half, keys[: 2 * SEAM], keys[side - 2 * SEAM :])

    values_ref[...] = mm_t(
        t2i_qkv_ref[:, 2 * inner :].astype(f32).T.astype(bf16), cells_ref[...]
    ).astype(bf16)
    tokens = start.shape[0]
    for at in range(0, HEADS * tokens, PROBES_AT_ONCE):
        probe = probes[at : at + PROBES_AT_ONCE]
        rows = slice(
            at // tokens * head_width, ((at + PROBES_AT_ONCE - 1) // tokens + 1) * head_width
        )
        for cell in range(0, pixels, KEYS_AT_ONCE):
            near = slice(cell, cell + KEYS_AT_ONCE)
            raw = mm_t(keys_ref[near, :], probe)
            top = jnp.max(raw, axis=0, keepdims=True)
            if cell > 0:
                top = jnp.maximum(top, old_top)
                fade = jnp.exp2(old_top - top)
            raw = jnp.exp2(raw - top)
            total = jnp.sum(raw, axis=0, keepdims=True)
            pooled = mm(values_ref[rows, near], raw.astype(bf16))
            if cell > 0:
                total = total + fade * old_total
                pooled = pooled + fade * old_pooled
            old_top, old_total, old_pooled = top, total, pooled
        pooled_ref[rows, at : at + PROBES_AT_ONCE] = pooled / total
    joined = jnp.concatenate(
        [
            pooled_ref[h * head_width : (h + 1) * head_width, h * tokens : (h + 1) * tokens]
            for h in range(HEADS)
        ],
        axis=0,
    ).T
    queries = layer_norm(queries + wide_mm(joined, t2i_out_ref[...]), gains_ref[1:2])
    hidden = jnp.maximum(wide_mm(queries, mlp_up_ref[...]), 0.0)
    queries = layer_norm(queries + wide_mm(hidden, mlp_down_ref[...]), gains_ref[2:3])

    back_k = wide_mm(queries + start, i2t_qkv_ref[:, inner : 2 * inner])
    back_v = wide_mm(queries, i2t_qkv_ref[:, 2 * inner :])
    gaps = by_group(back_k[:slots] - back_k[slots:], inner)
    gaps = wide_mm(gaps, i2t_qkv_ref[:, :inner], mm_t) * (0.5 * head_scale)
    gaps = gaps.astype(bf16)
    middle = 0.5 * (back_v[:slots] + back_v[slots:])
    apart = by_group(0.5 * (back_v[:slots] - back_v[slots:]), inner)
    moves = wide_mm(jnp.concatenate([apart, middle], axis=0), i2t_out_ref[...])
    moves = (moves - jnp.mean(moves, axis=1, keepdims=True)).astype(bf16)
    hyper = wide_mm(jnp.maximum(wide_mm(queries[:slots], hyper_ref[0]), 0.0), hyper_ref[1])
    hyper = hyper.astype(bf16).astype(f32) * gains_ref[3:4]
    hyper = (hyper - jnp.mean(hyper, axis=1, keepdims=True)).astype(bf16)
    apart, middle = moves[: HEADS * slots], moves[HEADS * slots :]
    middle_wide, hyper_wide = middle.astype(f32), hyper.astype(f32)
    consts = jnp.concatenate(
        [
            jnp.sum(middle_wide * middle_wide, axis=1, keepdims=True),
            jnp.sum(middle_wide * hyper_wide, axis=1, keepdims=True),
        ],
        axis=1,
    )
    block = HEADS * SLOT_GROUP
    tall = block + 2 * SLOT_GROUP
    row_slot = lax.rem(lax.broadcasted_iota(jnp.int32, (tall, block), 0), SLOT_GROUP)
    column_slot = lax.rem(lax.broadcasted_iota(jnp.int32, (tall, block), 1), SLOT_GROUP)
    on_cells, on_weights = [], []
    for at in range(0, slots, SLOT_GROUP):
        mine = apart[at * HEADS : (at + SLOT_GROUP) * HEADS]
        mine_twice = (2.0 * mine.astype(f32)).astype(bf16)
        centre_twice = (2.0 * middle_wide[at : at + SLOT_GROUP]).astype(bf16)
        mask = hyper[at : at + SLOT_GROUP]
        on_cells += [mine_twice, centre_twice, mask]
        crossed = mm_t(jnp.concatenate([mine, centre_twice, mask], axis=0), mine)
        on_weights.append(jnp.where(row_slot == column_slot, crossed, 0.0).astype(bf16))
    on_cells.append(jnp.ones((SLOT_GROUP, width), bf16))
    on_cells = jnp.concatenate(on_cells, axis=0)
    on_weights = jnp.concatenate(on_weights, axis=0)
    gaps_ref[...] = gaps
    on_cells_ref[...] = on_cells
    on_weights_ref[...] = on_weights
    consts_ref[...] = consts

    weights = cell_weights(gaps, seam_keys_ref[...].astype(bf16))
    _, covers = cell_logits(
        weights, seam_cells_ref[...].astype(bf16), on_cells, on_weights, consts, live
    )
    count = 2 * SEAM * side
    line = lax.broadcasted_iota(jnp.int32, (side, count), 0)
    column = lax.broadcasted_iota(jnp.int32, (side, count), 1)
    near = (column >= line * 2 * SEAM) & (column < (line + 1) * 2 * SEAM)
    ours = lax.rem(lax.broadcasted_iota(jnp.int32, (count, side), 0), 2 * SEAM)
    theirs = lax.broadcasted_iota(jnp.int32, (count, side), 1)
    left = jnp.where(ours < SEAM, SEAM + 1 - (side + ours - theirs), 0)
    right = jnp.where(ours >= SEAM, SEAM + 1 - (theirs + 2 * SEAM - ours), 0)
    lines = jnp.where(near, covers, 0.0)
    scale = 1.0 / (SEAM + 1) ** 2
    to_left_ref[...] = scale * wide_mm(lines, jnp.maximum(left, 0).astype(f32).astype(bf16))
    to_right_ref[...] = scale * wide_mm(lines, jnp.maximum(right, 0).astype(f32).astype(bf16))


def image_kernel(
    counts_ref,
    cells_ref,
    keys_ref,
    gaps_ref,
    on_cells_ref,
    on_weights_ref,
    consts_ref,
    logits_ref,
    blended_ref,
    coverage_ref,
):
    pixels, width = cells_ref.shape
    side = math.isqrt(pixels)
    live = counts_ref[0, lax.axis_index("row")]
    gaps, on_cells, on_weights = gaps_ref[...], on_cells_ref[...], on_weights_ref[...]
    consts = consts_ref[...]
    places = [slice(at, at + CELLS_AT_ONCE) for at in range(0, pixels, CELLS_AT_ONCE)]
    weights = cell_weights(gaps, keys_ref[places[0], :])
    for step, place in enumerate(places):
        now = weights
        if step + 1 < len(places):
            weights = cell_weights(gaps, keys_ref[places[step + 1], :])
        logits, covers = cell_logits(now, cells_ref[place, :], on_cells, on_weights, consts, live)
        logits_ref[:, place] = logits
        for at in range(0, CELLS_AT_ONCE, side):
            line = (step * CELLS_AT_ONCE + at) // side
            coverage_ref[line : line + 1, :] = covers[:, at : at + side]
    apart = jnp.abs(
        lax.broadcasted_iota(jnp.int32, (side, side), 0)
        - lax.broadcasted_iota(jnp.int32, (side, side), 1)
    )
    band = jnp.maximum(SEAM + 1 - apart, 0).astype(f32).astype(bf16)
    blended_ref[...] = (1.0 / (SEAM + 1) ** 2) * wide_mm(coverage_ref[...], band)


def shards(
    embedding,
    counts,
    points,
    pe_gauss,
    point_embed,
    mask_token,
    sa_qkv,
    sa_out,
    t2i_qkv,
    t2i_out,
    mlp_up,
    mlp_down,
    i2t_qkv,
    i2t_out,
    hyper_w,
    ln_gains,
):
    side = embedding.shape[0]
    width = embedding.shape[2]
    inner = t2i_qkv.shape[1] // 3
    slots = points.shape[3]
    pixels = side * side
    groups = slots // SLOT_GROUP
    tall = (HEADS + 2) * SLOT_GROUP
    whole = pl.BlockSpec(memory_space=pltpu.VMEM)
    scalars = pl.BlockSpec(memory_space=pltpu.SMEM)
    cells = embedding.reshape(pixels, width)
    shape = jax.ShapeDtypeStruct
    params = pltpu.CompilerParams(vmem_limit_bytes=58 << 20)
    *slot_side, to_left, to_right = pl.pallas_call(
        decode_kernel,
        out_shape=(
            shape((pixels, width), bf16),
            shape((HEADS * slots, width), bf16),
            shape((groups * tall + SLOT_GROUP, width), bf16),
            shape((groups * tall, HEADS * SLOT_GROUP), bf16),
            shape((slots, 2), f32),
            shape((side, side), f32),
            shape((side, side), f32),
        ),
        in_specs=[scalars] + [whole] * 15,
        out_specs=(whole,) * 7,
        scratch_shapes=[
            pltpu.VMEM((2 * SEAM * side, width), f32),
            pltpu.VMEM((2 * SEAM * side, width), f32),
            pltpu.VMEM((inner, pixels), bf16),
            pltpu.VMEM((inner, 2 * slots * HEADS), f32),
        ],
        compiler_params=params,
        name="decode",
    )(
        counts,
        points.reshape(2, slots),
        pe_gauss,
        point_embed.reshape(1, width),
        mask_token.reshape(1, width),
        sa_qkv,
        sa_out,
        t2i_qkv,
        t2i_out,
        mlp_up,
        mlp_down,
        i2t_qkv,
        i2t_out,
        hyper_w,
        ln_gains,
        cells,
    )
    count = lax.axis_size("col")
    from_right = lax.ppermute(to_left, "col", [(i + 1, i) for i in range(count - 1)])
    from_left = lax.ppermute(to_right, "col", [(i, i + 1) for i in range(count - 1)])
    logits, blended = pl.pallas_call(
        image_kernel,
        out_shape=(shape((slots, pixels), bf16), shape((side, side), f32)),
        in_specs=[scalars] + [whole] * 6,
        out_specs=(whole,) * 2,
        scratch_shapes=[pltpu.VMEM((side, side), f32)],
        compiler_params=params,
        name="image",
    )(counts, cells, *slot_side)
    return (logits.reshape(1, 1, slots, pixels), blended + from_left + from_right)


def solution(mesh):
    placed = (P("row", "col", None), P("col", None), P("row", "col", None, None)) + (P(),) * 13
    return jax.shard_map(
        shards,
        mesh=mesh,
        in_specs=placed,
        out_specs=(P("row", "col", None, None), P("row", "col")),
        check_vma=False,
    )
```

```python
import functools
import math

import jax
import jax.numpy as jnp
from jax import lax
from jax.experimental import pallas as pl
from jax.experimental.pallas import tpu as pltpu
from jax.sharding import PartitionSpec as P

HEADS = 8
SEAM = 4
IMG = 1024
SLOT_GROUP = 16
KEYS_AT_ONCE = 512
PROBES_AT_ONCE = 256
FOLD = 64
ARRAYS = 16
FETCH_ORDER = (2, 1, 4, 3, 14, 5, 6, 7, 15, 8, 9, 10, 11, 12, 13, 0)
CELLS_AT_ONCE = 512

norm_eps = 1e-05
bf16 = jnp.bfloat16
f32 = jnp.float32


def mm(left, right):
    return lax.dot_general(left, right, (((1,), (0,)), ((), ())), preferred_element_type=f32)


def mm_t(left, right):
    return lax.dot_general(left, right, (((1,), (1,)), ((), ())), preferred_element_type=f32)


def halves(values):
    high = values.astype(bf16)
    low = (values - high.astype(f32)).astype(bf16)
    return jnp.concatenate([high, low], axis=0)


def wide_mm(values, weight, product=mm):
    rows = values.shape[0]
    both = product(halves(values), weight)
    return both[:rows] + both[rows:]


def layer_norm(values, gain):
    centred = values - jnp.mean(values, axis=-1, keepdims=True)
    spread = jnp.mean(centred * centred, axis=-1, keepdims=True)
    return centred * lax.rsqrt(spread + norm_eps) * gain


def sin_turns(turns):
    part = turns - jnp.floor(turns + 0.5)
    size = 0.25 - jnp.abs(jnp.abs(part) - 0.25)
    angle = (2.0 * math.pi) * jnp.where(part < 0.0, -size, size)
    square = angle * angle
    total = jnp.full_like(angle, -1.0 / math.factorial(11))
    for order in (9, 7, 5, 3, 1):
        sign = 1.0 if order % 4 == 1 else -1.0
        total = total * square + sign / math.factorial(order)
    return total * angle


def fold_rows(values, join):
    total = values[:FOLD]
    for at in range(FOLD, values.shape[0], FOLD):
        total = join(total, values[at : at + FOLD])
    rows = FOLD
    while rows > 1:
        rows //= 2
        total = join(total[:rows], total[rows:])
    return total


def by_head(rows, inner_width):
    head_width = inner_width // HEADS
    lane = lax.broadcasted_iota(jnp.int32, rows.shape, 1)
    return jnp.concatenate(
        [
            jnp.where((lane >= h * head_width) & (lane < (h + 1) * head_width), rows, 0.0)
            for h in range(HEADS)
        ],
        axis=0,
    )


def by_group(rows, inner_width):
    return jnp.concatenate(
        [
            by_head(rows[at : at + SLOT_GROUP], inner_width)
            for at in range(0, rows.shape[0], SLOT_GROUP)
        ],
        axis=0,
    )


def group_ones(width, group):
    row = lax.broadcasted_iota(jnp.int32, (width, width), 0)
    column = lax.broadcasted_iota(jnp.int32, (width, width), 1)
    first = row - lax.rem(row, group)
    return jnp.where((column >= first) & (column < first + group), 1.0, 0.0).astype(bf16)


def cell_weights(gaps, keys):
    return jnp.tanh(mm_t(gaps, keys)).astype(bf16)


def cell_logits(weights, cells, on_cells, on_weights, consts, live):
    count, width = cells.shape
    slots = consts.shape[0]
    block = HEADS * SLOT_GROUP
    tall = block + 2 * SLOT_GROUP
    flat = mm_t(on_cells, cells)
    wide = cells.astype(f32)
    norms = mm_t(jnp.ones((SLOT_GROUP, width), bf16), halves(wide * wide))
    total = flat[slots // SLOT_GROUP * tall :][:SLOT_GROUP]
    norms = norms[:, :count] + norms[:, count:] - total * total * (1.0 / width)
    logits, covers = [], []
    for at in range(0, slots, SLOT_GROUP):
        group = at // SLOT_GROUP
        mine = weights[group * block : (group + 1) * block]
        both = flat[group * tall : (group + 1) * tall] + mm(
            on_weights[group * tall : (group + 1) * tall], mine
        )
        square = norms + both[block : block + SLOT_GROUP] + consts[at : at + SLOT_GROUP, 0:1]
        for h in range(HEADS):
            part = slice(h * SLOT_GROUP, (h + 1) * SLOT_GROUP)
            square = square + mine[part].astype(f32) * both[part]
        dots = both[block + SLOT_GROUP :] + consts[at : at + SLOT_GROUP, 1:2]
        kept = at + lax.broadcasted_iota(jnp.int32, (SLOT_GROUP, count), 0) < live
        found = dots * lax.rsqrt(jnp.maximum(square, 0.0) + width * norm_eps)
        found = jnp.where(kept, found, 0.0).astype(bf16)
        logits.append(found)
        covers.append(jnp.where(kept, 0.5 * jnp.tanh(0.5 * found.astype(f32)) + 0.5, 0.0))
    return jnp.concatenate(logits, axis=0), jnp.sum(sum(covers), axis=0, keepdims=True)


def decode_kernel(*refs):
    far, refs = refs[:ARRAYS], refs[ARRAYS:]
    (cells_ref, *slot_side), refs = refs[:8], refs[8:]
    near, (sems, *scratch) = refs[: ARRAYS - 1], refs[ARRAYS - 1 :]
    near = [*near, cells_ref]
    copies = [pltpu.make_async_copy(*pair, sems.at[at]) for at, pair in enumerate(zip(far, near))]
    for at in FETCH_ORDER:
        copies[at].start()
    decode(copies, *near, *slot_side, *scratch)


def decode(
    copies,
    counts_ref,
    points_ref,
    gauss_ref,
    point_embed_ref,
    mask_token_ref,
    sa_qkv_ref,
    sa_out_ref,
    t2i_qkv_ref,
    t2i_out_ref,
    mlp_up_ref,
    mlp_down_ref,
    i2t_qkv_ref,
    i2t_out_ref,
    hyper_ref,
    gains_ref,
    cells_ref,
    keys_ref,
    gaps_ref,
    on_cells_ref,
    on_weights_ref,
    consts_ref,
    even_ref,
    odd_ref,
    seam_cells_ref,
    seam_keys_ref,
    values_ref,
    pooled_ref,
):
    pixels, width = cells_ref.shape
    side = math.isqrt(pixels)
    slots = points_ref.shape[1]
    inner = t2i_qkv_ref.shape[1] // 3
    head_width = inner // HEADS
    half = width // 2
    for at in FETCH_ORDER[:5]:
        copies[at].wait()

    gauss = gauss_ref[...]
    steps = lax.broadcasted_iota(jnp.int32, (side, half), 0).astype(f32)
    steps = (2.0 * (steps + 0.5)) / side - 1.0
    spots = jnp.clip(points_ref[...], 0, IMG - 1).astype(f32)
    spots = 2.0 * ((spots + 0.5) / IMG) - 1.0
    same = lax.broadcasted_iota(jnp.int32, (slots, slots), 0) == lax.broadcasted_iota(
        jnp.int32, (slots, slots), 1
    )
    spot_x = jnp.sum(jnp.where(same, spots[0:1], 0.0), axis=1, keepdims=True)
    spot_y = jnp.sum(jnp.where(same, spots[1:2], 0.0), axis=1, keepdims=True)
    turns = jnp.concatenate(
        [steps * gauss[0:1], steps * gauss[1:2], spot_x * gauss[0:1] + spot_y * gauss[1:2]], axis=0
    )
    sines = sin_turns(turns)
    cosines = sin_turns(turns + 0.25)
    prompt = jnp.concatenate([sines[2 * side :], cosines[2 * side :]], axis=1)

    start = jnp.concatenate(
        [
            jnp.broadcast_to(mask_token_ref[...], (slots, width)),
            prompt + point_embed_ref[...],
        ],
        axis=0,
    )
    for at in FETCH_ORDER[5:8]:
        copies[at].wait()
    qkv = wide_mm(start, sa_qkv_ref[...])
    query, key, value = qkv[:, :width], qkv[:, width : 2 * width], qkv[:, 2 * width :]
    key_gap = key[:slots] - key[slots:]
    value_gap = value[:slots] - value[slots:]
    scores = wide_mm(
        query * jnp.concatenate([key_gap, key_gap], axis=0), group_ones(width, width // HEADS)
    )
    first = 0.5 * jnp.tanh((0.5 / math.sqrt(width // HEADS)) * scores) + 0.5
    attended = jnp.concatenate([value[slots:]] * 2, axis=0) + first * jnp.concatenate(
        [value_gap, value_gap], axis=0
    )
    queries = layer_norm(wide_mm(attended, sa_out_ref[...]), gains_ref[0:1])
    head_scale = 1.0 / math.sqrt(head_width)
    cross_q = wide_mm(queries + start, t2i_qkv_ref[:, :inner])
    cross_q = by_head(cross_q, inner).astype(bf16)
    probes = mm_t(cross_q, t2i_qkv_ref[:, inner : 2 * inner]) * (head_scale * math.log2(math.e))
    probes = probes.astype(bf16)

    copies[FETCH_ORDER[8]].wait()
    sin_x, cos_x = sines[:side], cosines[:side]
    left_half = lax.broadcasted_iota(jnp.int32, (2 * SEAM, width), 0) < SEAM
    for line in range(side):
        sin_y, cos_y = sines[side + line : side + line + 1], cosines[side + line : side + line + 1]
        place = slice(line * side, (line + 1) * side)
        encoding = jnp.concatenate(
            [sin_x * cos_y + cos_x * sin_y, cos_x * cos_y - sin_x * sin_y], axis=1
        )
        own = cells_ref[place, :].astype(f32)
        keys = own + encoding
        keys_ref[place, :] = keys.astype(bf16)
        seam = slice(line * 2 * SEAM, (line + 1) * 2 * SEAM)
        seam_cells_ref[seam, :] = jnp.where(left_half, own[: 2 * SEAM], own[side - 2 * SEAM :])
        seam_keys_ref[seam, :] = jnp.where(left_half, keys[: 2 * SEAM], keys[side - 2 * SEAM :])

    values_ref[...] = mm_t(
        t2i_qkv_ref[:, 2 * inner :].astype(f32).T.astype(bf16), cells_ref[...]
    ).astype(bf16)
    tokens = start.shape[0]
    def raw_scores(cell):
        return mm_t(keys_ref[cell : cell + KEYS_AT_ONCE, :], probes)

    ahead = raw_scores(0)
    for cell in range(0, pixels, KEYS_AT_ONCE):
        raw = ahead
        if cell + KEYS_AT_ONCE < pixels:
            ahead = raw_scores(cell + KEYS_AT_ONCE)
        top = fold_rows(raw, jnp.maximum)
        if cell > 0:
            top = jnp.maximum(top, old_top)
            fade = jnp.exp2(old_top - top)
        raw = jnp.exp2(raw - top)
        total = fold_rows(raw, jnp.add)
        raw = raw.astype(bf16)
        if cell > 0:
            total = total + fade * old_total
        for at in range(0, HEADS * tokens, PROBES_AT_ONCE):
            rows = slice(
                at // tokens * head_width, ((at + PROBES_AT_ONCE - 1) // tokens + 1) * head_width
            )
            lanes = slice(at, at + PROBES_AT_ONCE)
            pooled = mm(values_ref[rows, cell : cell + KEYS_AT_ONCE], raw[:, lanes])
            if cell > 0:
                pooled = pooled + fade[:, lanes] * pooled_ref[rows, lanes]
            if cell + KEYS_AT_ONCE == pixels:
                pooled = pooled / total[:, lanes]
            pooled_ref[rows, lanes] = pooled
        old_top, old_total = top, total
    joined = jnp.concatenate(
        [
            pooled_ref[h * head_width : (h + 1) * head_width, h * tokens : (h + 1) * tokens]
            for h in range(HEADS)
        ],
        axis=0,
    ).T
    for at in FETCH_ORDER[9:]:
        copies[at].wait()
    queries = layer_norm(queries + wide_mm(joined, t2i_out_ref[...]), gains_ref[1:2])
    hidden = jnp.maximum(wide_mm(queries, mlp_up_ref[...]), 0.0)
    queries = layer_norm(queries + wide_mm(hidden, mlp_down_ref[...]), gains_ref[2:3])

    back_k = wide_mm(queries + start, i2t_qkv_ref[:, inner : 2 * inner])
    back_v = wide_mm(queries, i2t_qkv_ref[:, 2 * inner :])
    gaps = by_group(back_k[:slots] - back_k[slots:], inner)
    gaps = wide_mm(gaps, i2t_qkv_ref[:, :inner], mm_t) * (0.5 * head_scale)
    gaps = gaps.astype(bf16)
    middle = 0.5 * (back_v[:slots] + back_v[slots:])
    apart = by_group(0.5 * (back_v[:slots] - back_v[slots:]), inner)
    moves = wide_mm(jnp.concatenate([apart, middle], axis=0), i2t_out_ref[...])
    moves = (moves - jnp.mean(moves, axis=1, keepdims=True)).astype(bf16)
    hyper = wide_mm(jnp.maximum(wide_mm(queries[:slots], hyper_ref[0]), 0.0), hyper_ref[1])
    hyper = hyper.astype(bf16).astype(f32) * gains_ref[3:4]
    hyper = (hyper - jnp.mean(hyper, axis=1, keepdims=True)).astype(bf16)
    apart, middle = moves[: HEADS * slots], moves[HEADS * slots :]
    middle_wide, hyper_wide = middle.astype(f32), hyper.astype(f32)
    consts = jnp.concatenate(
        [
            jnp.sum(middle_wide * middle_wide, axis=1, keepdims=True),
            jnp.sum(middle_wide * hyper_wide, axis=1, keepdims=True),
        ],
        axis=1,
    )
    block = HEADS * SLOT_GROUP
    tall = block + 2 * SLOT_GROUP
    row_slot = lax.rem(lax.broadcasted_iota(jnp.int32, (tall, block), 0), SLOT_GROUP)
    column_slot = lax.rem(lax.broadcasted_iota(jnp.int32, (tall, block), 1), SLOT_GROUP)
    on_cells, on_weights = [], []
    for at in range(0, slots, SLOT_GROUP):
        mine = apart[at * HEADS : (at + SLOT_GROUP) * HEADS]
        mine_twice = (2.0 * mine.astype(f32)).astype(bf16)
        centre_twice = (2.0 * middle_wide[at : at + SLOT_GROUP]).astype(bf16)
        mask = hyper[at : at + SLOT_GROUP]
        on_cells += [mine_twice, centre_twice, mask]
        crossed = mm_t(jnp.concatenate([mine, centre_twice, mask], axis=0), mine)
        on_weights.append(jnp.where(row_slot == column_slot, crossed, 0.0).astype(bf16))
    on_cells.append(jnp.ones((SLOT_GROUP, width), bf16))
    on_cells = jnp.concatenate(on_cells, axis=0)
    on_weights = jnp.concatenate(on_weights, axis=0)
    gaps_ref[...] = gaps
    on_cells_ref[...] = on_cells
    on_weights_ref[...] = on_weights
    consts_ref[...] = consts

    live = counts_ref[0, lax.axis_index("row")]
    weights = cell_weights(gaps, seam_keys_ref[...].astype(bf16))
    _, covers = cell_logits(
        weights, seam_cells_ref[...].astype(bf16), on_cells, on_weights, consts, live
    )
    count = 2 * SEAM * side
    line = lax.broadcasted_iota(jnp.int32, (side, count), 0)
    column = lax.broadcasted_iota(jnp.int32, (side, count), 1)
    near = (column >= line * 2 * SEAM) & (column < (line + 1) * 2 * SEAM)
    ours = lax.rem(lax.broadcasted_iota(jnp.int32, (count, side), 0), 2 * SEAM)
    theirs = lax.broadcasted_iota(jnp.int32, (count, side), 1)
    left = jnp.where(ours < SEAM, SEAM + 1 - (side + ours - theirs), 0)
    right = jnp.where(ours >= SEAM, SEAM + 1 - (theirs + 2 * SEAM - ours), 0)
    lines = jnp.where(near, covers, 0.0)
    scale = 1.0 / (SEAM + 1) ** 2
    to_left = scale * wide_mm(lines, jnp.maximum(left, 0).astype(f32).astype(bf16))
    to_right = scale * wide_mm(lines, jnp.maximum(right, 0).astype(f32).astype(bf16))
    even = lax.rem(lax.axis_index("col"), 2) == 0
    even_ref[...] = jnp.where(even, to_right, to_left)
    odd_ref[...] = jnp.where(even, to_left, to_right)


def image_kernel(
    counts_ref,
    cells_ref,
    keys_ref,
    gaps_ref,
    on_cells_ref,
    on_weights_ref,
    consts_ref,
    logits_ref,
    blended_ref,
    coverage_ref,
    found_ref,
    sems,
):
    pixels, width = cells_ref.shape
    side = math.isqrt(pixels)
    live = counts_ref[0, lax.axis_index("row")]
    gaps, on_cells, on_weights = gaps_ref[...], on_cells_ref[...], on_weights_ref[...]
    consts = consts_ref[...]
    places = [slice(at, at + CELLS_AT_ONCE) for at in range(0, pixels, CELLS_AT_ONCE)]
    weights = cell_weights(gaps, keys_ref[places[0], :])
    copies = []
    for step, place in enumerate(places):
        now = weights
        if step + 1 < len(places):
            weights = cell_weights(gaps, keys_ref[places[step + 1], :])
        logits, covers = cell_logits(now, cells_ref[place, :], on_cells, on_weights, consts, live)
        found_ref[:, place] = logits
        copies.append(
            pltpu.make_async_copy(found_ref.at[:, place], logits_ref.at[:, place], sems.at[step])
        )
        copies[-1].start()
        for at in range(0, CELLS_AT_ONCE, side):
            line = (step * CELLS_AT_ONCE + at) // side
            coverage_ref[line : line + 1, :] = covers[:, at : at + side]
    apart = jnp.abs(
        lax.broadcasted_iota(jnp.int32, (side, side), 0)
        - lax.broadcasted_iota(jnp.int32, (side, side), 1)
    )
    band = jnp.maximum(SEAM + 1 - apart, 0).astype(f32).astype(bf16)
    blended_ref[...] = (1.0 / (SEAM + 1) ** 2) * wide_mm(coverage_ref[...], band)
    for copy in copies:
        copy.wait()


def shards(
    embedding,
    counts,
    points,
    pe_gauss,
    point_embed,
    mask_token,
    sa_qkv,
    sa_out,
    t2i_qkv,
    t2i_out,
    mlp_up,
    mlp_down,
    i2t_qkv,
    i2t_out,
    hyper_w,
    ln_gains,
):
    side = embedding.shape[0]
    width = embedding.shape[2]
    inner = t2i_qkv.shape[1] // 3
    slots = points.shape[3]
    pixels = side * side
    groups = slots // SLOT_GROUP
    tall = (HEADS + 2) * SLOT_GROUP
    whole = pl.BlockSpec(memory_space=pltpu.VMEM)
    scalars = pl.BlockSpec(memory_space=pltpu.SMEM)
    cells = embedding.reshape(pixels, width)
    shape = jax.ShapeDtypeStruct
    params = pltpu.CompilerParams(vmem_limit_bytes=36 << 20)
    far = pl.BlockSpec(memory_space=pltpu.HBM)
    arrays = [
        pltpu.with_memory_space_constraint(one, pltpu.HBM)
        for one in (
            counts,
            points.reshape(2, slots),
            pe_gauss,
            point_embed.reshape(1, width),
            mask_token.reshape(1, width),
            sa_qkv,
            sa_out,
            t2i_qkv,
            t2i_out,
            mlp_up,
            mlp_down,
            i2t_qkv,
            i2t_out,
            hyper_w,
            ln_gains,
            cells,
        )
    ]
    *slot_side, even, odd = pl.pallas_call(
        decode_kernel,
        out_shape=(
            shape((pixels, width), bf16),
            shape((pixels, width), bf16),
            shape((HEADS * slots, width), bf16),
            shape((groups * tall + SLOT_GROUP, width), bf16),
            shape((groups * tall, HEADS * SLOT_GROUP), bf16),
            shape((slots, 2), f32),
            shape((side, side), f32),
            shape((side, side), f32),
        ),
        in_specs=[far] * ARRAYS,
        out_specs=(whole,) * 8,
        scratch_shapes=[pltpu.SMEM(counts.shape, counts.dtype)]
        + [pltpu.VMEM(one.shape, one.dtype) for one in arrays[1:-1]]
        + [
            pltpu.SemaphoreType.DMA((ARRAYS,)),
            pltpu.VMEM((2 * SEAM * side, width), f32),
            pltpu.VMEM((2 * SEAM * side, width), f32),
            pltpu.VMEM((inner, pixels), bf16),
            pltpu.VMEM((inner, 2 * slots * HEADS), f32),
        ],
        compiler_params=params,
        name="decode",
    )(*arrays)
    count = lax.axis_size("col")
    swaps = [
        [pair for i in range(first, count - 1, 2) for pair in ((i, i + 1), (i + 1, i))]
        for first in (0, 1)
    ]
    odd = lax.ppermute(odd, "col", swaps[1])
    even = lax.ppermute(even, "col", swaps[0])
    logits, blended = pl.pallas_call(
        image_kernel,
        out_shape=(shape((slots, pixels), bf16), shape((side, side), f32)),
        in_specs=[scalars] + [whole] * 6,
        out_specs=(pl.BlockSpec(memory_space=pltpu.HBM), whole),
        scratch_shapes=[
            pltpu.VMEM((side, side), f32),
            pltpu.VMEM((slots, pixels), bf16),
            pltpu.SemaphoreType.DMA((pixels // CELLS_AT_ONCE,)),
        ],
        compiler_params=params,
        name="image",
    )(arrays[0], *slot_side)
    return (logits.reshape(1, 1, slots, pixels), blended + odd + even)


def solution(mesh):
    placed = (P("row", "col", None), P("col", None), P("row", "col", None, None)) + (P(),) * 13
    return jax.shard_map(
        shards,
        mesh=mesh,
        in_specs=placed,
        out_specs=(P("row", "col", None, None), P("row", "col")),
        check_vma=False,
    )
```

```python
import functools
import math

import jax
import jax.numpy as jnp
from jax import lax
from jax.experimental import pallas as pl
from jax.experimental.pallas import tpu as pltpu
from jax.sharding import PartitionSpec as P

HEADS = 8
SEAM = 4
IMG = 1024
SLOT_GROUP = 16
KEYS_AT_ONCE = 512
PROBES_AT_ONCE = 256
FOLD = 64
ARRAYS = 16
FETCH_ORDER = (2, 1, 4, 3, 14, 5, 6, 7, 15, 8, 9, 10, 11, 12, 13, 0)
CELLS_AT_ONCE = 512

norm_eps = 1e-05
bf16 = jnp.bfloat16
f32 = jnp.float32


def mm(left, right):
    return lax.dot_general(left, right, (((1,), (0,)), ((), ())), preferred_element_type=f32)


def mm_t(left, right):
    return lax.dot_general(left, right, (((1,), (1,)), ((), ())), preferred_element_type=f32)


def halves(values):
    high = values.astype(bf16)
    low = (values - high.astype(f32)).astype(bf16)
    return jnp.concatenate([high, low], axis=0)


def wide_mm(values, weight, product=mm):
    rows = values.shape[0]
    both = product(halves(values), weight)
    return both[:rows] + both[rows:]


def token_mm(values, weight):
    return mm(values.astype(bf16), weight)


def layer_norm(values, gain):
    centred = values - jnp.mean(values, axis=-1, keepdims=True)
    spread = jnp.mean(centred * centred, axis=-1, keepdims=True)
    return centred * lax.rsqrt(spread + norm_eps) * gain


def sin_turns(turns):
    part = turns - jnp.floor(turns + 0.5)
    size = 0.25 - jnp.abs(jnp.abs(part) - 0.25)
    angle = (2.0 * math.pi) * jnp.where(part < 0.0, -size, size)
    square = angle * angle
    total = jnp.full_like(angle, -1.0 / math.factorial(11))
    for order in (9, 7, 5, 3, 1):
        sign = 1.0 if order % 4 == 1 else -1.0
        total = total * square + sign / math.factorial(order)
    return total * angle


def fold_rows(values, join):
    total = values[:FOLD]
    for at in range(FOLD, values.shape[0], FOLD):
        total = join(total, values[at : at + FOLD])
    rows = FOLD
    while rows > 1:
        rows //= 2
        total = join(total[:rows], total[rows:])
    return total


def by_head(rows, inner_width):
    head_width = inner_width // HEADS
    lane = lax.broadcasted_iota(jnp.int32, rows.shape, 1)
    return jnp.concatenate(
        [
            jnp.where((lane >= h * head_width) & (lane < (h + 1) * head_width), rows, 0.0)
            for h in range(HEADS)
        ],
        axis=0,
    )


def by_group(rows, inner_width):
    return jnp.concatenate(
        [
            by_head(rows[at : at + SLOT_GROUP], inner_width)
            for at in range(0, rows.shape[0], SLOT_GROUP)
        ],
        axis=0,
    )


def group_ones(width, group):
    row = lax.broadcasted_iota(jnp.int32, (width, width), 0)
    column = lax.broadcasted_iota(jnp.int32, (width, width), 1)
    first = row - lax.rem(row, group)
    return jnp.where((column >= first) & (column < first + group), 1.0, 0.0).astype(bf16)


def cell_weights(gaps, keys):
    return jnp.tanh(mm_t(gaps, keys)).astype(bf16)


def cell_logits(weights, cells, on_cells, on_weights, consts, live):
    count, width = cells.shape
    slots = consts.shape[0]
    block = HEADS * SLOT_GROUP
    tall = block + 2 * SLOT_GROUP
    flat = mm_t(on_cells, cells)
    wide = cells.astype(f32)
    norms = jnp.sum(wide * wide, axis=1, keepdims=True)
    lanes = 128
    same = lax.broadcasted_iota(jnp.int32, (lanes, lanes), 0) == lax.broadcasted_iota(
        jnp.int32, (lanes, lanes), 1
    )
    norms = jnp.concatenate(
        [
            jnp.sum(jnp.where(same, norms[at : at + lanes], 0.0), axis=0, keepdims=True)
            for at in range(0, count, lanes)
        ],
        axis=1,
    )
    total = flat[slots // SLOT_GROUP * tall :][:SLOT_GROUP]
    norms = norms - total * total * (1.0 / width)
    logits, covers = [], []
    for at in range(0, slots, SLOT_GROUP):
        group = at // SLOT_GROUP
        mine = weights[group * block : (group + 1) * block]
        both = flat[group * tall : (group + 1) * tall] + mm(
            on_weights[group * tall : (group + 1) * tall], mine
        )
        square = norms + both[block : block + SLOT_GROUP] + consts[at : at + SLOT_GROUP, 0:1]
        for h in range(HEADS):
            part = slice(h * SLOT_GROUP, (h + 1) * SLOT_GROUP)
            square = square + mine[part].astype(f32) * both[part]
        dots = both[block + SLOT_GROUP :] + consts[at : at + SLOT_GROUP, 1:2]
        kept = at + lax.broadcasted_iota(jnp.int32, (SLOT_GROUP, count), 0) < live
        found = dots * lax.rsqrt(jnp.maximum(square, 0.0) + width * norm_eps)
        found = jnp.where(kept, found, 0.0).astype(bf16)
        logits.append(found)
        covers.append(jnp.where(kept, 0.5 * jnp.tanh(0.5 * found.astype(f32)) + 0.5, 0.0))
    return jnp.concatenate(logits, axis=0), jnp.sum(sum(covers), axis=0, keepdims=True)


def decode_kernel(*refs):
    far, refs = refs[:ARRAYS], refs[ARRAYS:]
    (cells_ref, *slot_side), refs = refs[:8], refs[8:]
    near, (sems, *scratch) = refs[: ARRAYS - 1], refs[ARRAYS - 1 :]
    near = [*near, cells_ref]
    copies = [pltpu.make_async_copy(*pair, sems.at[at]) for at, pair in enumerate(zip(far, near))]
    for at in FETCH_ORDER:
        copies[at].start()
    decode(copies, *near, *slot_side, *scratch)


def decode(
    copies,
    counts_ref,
    points_ref,
    gauss_ref,
    point_embed_ref,
    mask_token_ref,
    sa_qkv_ref,
    sa_out_ref,
    t2i_qkv_ref,
    t2i_out_ref,
    mlp_up_ref,
    mlp_down_ref,
    i2t_qkv_ref,
    i2t_out_ref,
    hyper_ref,
    gains_ref,
    cells_ref,
    keys_ref,
    gaps_ref,
    on_cells_ref,
    on_weights_ref,
    consts_ref,
    even_ref,
    odd_ref,
    seam_cells_ref,
    seam_keys_ref,
    values_ref,
    pooled_ref,
):
    pixels, width = cells_ref.shape
    side = math.isqrt(pixels)
    slots = points_ref.shape[1]
    inner = t2i_qkv_ref.shape[1] // 3
    head_width = inner // HEADS
    half = width // 2
    for at in FETCH_ORDER[:5]:
        copies[at].wait()

    gauss = gauss_ref[...]
    steps = lax.broadcasted_iota(jnp.int32, (side, half), 0).astype(f32)
    steps = (2.0 * (steps + 0.5)) / side - 1.0
    spots = jnp.clip(points_ref[...], 0, IMG - 1).astype(f32)
    spots = 2.0 * ((spots + 0.5) / IMG) - 1.0
    same = lax.broadcasted_iota(jnp.int32, (slots, slots), 0) == lax.broadcasted_iota(
        jnp.int32, (slots, slots), 1
    )
    spot_x = jnp.sum(jnp.where(same, spots[0:1], 0.0), axis=1, keepdims=True)
    spot_y = jnp.sum(jnp.where(same, spots[1:2], 0.0), axis=1, keepdims=True)
    turns = jnp.concatenate(
        [steps * gauss[0:1], steps * gauss[1:2], spot_x * gauss[0:1] + spot_y * gauss[1:2]], axis=0
    )
    sines = sin_turns(turns)
    cosines = sin_turns(turns + 0.25)
    prompt = jnp.concatenate([sines[2 * side :], cosines[2 * side :]], axis=1)

    start = jnp.concatenate(
        [
            jnp.broadcast_to(mask_token_ref[...], (slots, width)),
            prompt + point_embed_ref[...],
        ],
        axis=0,
    )
    for at in FETCH_ORDER[5:8]:
        copies[at].wait()
    qkv = wide_mm(start, sa_qkv_ref[...])
    query, key, value = qkv[:, :width], qkv[:, width : 2 * width], qkv[:, 2 * width :]
    key_gap = key[:slots] - key[slots:]
    value_gap = value[:slots] - value[slots:]
    scores = wide_mm(
        query * jnp.concatenate([key_gap, key_gap], axis=0), group_ones(width, width // HEADS)
    )
    first = 0.5 * jnp.tanh((0.5 / math.sqrt(width // HEADS)) * scores) + 0.5
    attended = jnp.concatenate([value[slots:]] * 2, axis=0) + first * jnp.concatenate(
        [value_gap, value_gap], axis=0
    )
    queries = layer_norm(wide_mm(attended, sa_out_ref[...]), gains_ref[0:1])
    head_scale = 1.0 / math.sqrt(head_width)
    cross_q = wide_mm(queries + start, t2i_qkv_ref[:, :inner])
    cross_q = by_head(cross_q, inner).astype(bf16)
    probes = mm_t(cross_q, t2i_qkv_ref[:, inner : 2 * inner]) * (head_scale * math.log2(math.e))
    probes = probes.astype(bf16)

    copies[FETCH_ORDER[8]].wait()
    sin_x, cos_x = sines[:side], cosines[:side]
    left_half = lax.broadcasted_iota(jnp.int32, (2 * SEAM, width), 0) < SEAM
    for line in range(side):
        sin_y, cos_y = sines[side + line : side + line + 1], cosines[side + line : side + line + 1]
        place = slice(line * side, (line + 1) * side)
        encoding = jnp.concatenate(
            [sin_x * cos_y + cos_x * sin_y, cos_x * cos_y - sin_x * sin_y], axis=1
        )
        own = cells_ref[place, :].astype(f32)
        keys = own + encoding
        keys_ref[place, :] = keys.astype(bf16)
        seam = slice(line * 2 * SEAM, (line + 1) * 2 * SEAM)
        seam_cells_ref[seam, :] = jnp.where(left_half, own[: 2 * SEAM], own[side - 2 * SEAM :])
        seam_keys_ref[seam, :] = jnp.where(left_half, keys[: 2 * SEAM], keys[side - 2 * SEAM :])

    values_ref[...] = mm_t(
        t2i_qkv_ref[:, 2 * inner :].astype(f32).T.astype(bf16), cells_ref[...]
    ).astype(bf16)
    tokens = start.shape[0]
    def raw_scores(cell):
        return mm_t(keys_ref[cell : cell + KEYS_AT_ONCE, :], probes)

    ahead = raw_scores(0)
    for cell in range(0, pixels, KEYS_AT_ONCE):
        raw = ahead
        if cell + KEYS_AT_ONCE < pixels:
            ahead = raw_scores(cell + KEYS_AT_ONCE)
        top = fold_rows(raw, jnp.maximum)
        if cell > 0:
            top = jnp.maximum(top, old_top)
            fade = jnp.exp2(old_top - top)
        raw = jnp.exp2(raw - top)
        total = fold_rows(raw, jnp.add)
        raw = raw.astype(bf16)
        if cell > 0:
            total = total + fade * old_total
        for at in range(0, HEADS * tokens, PROBES_AT_ONCE):
            rows = slice(
                at // tokens * head_width, ((at + PROBES_AT_ONCE - 1) // tokens + 1) * head_width
            )
            lanes = slice(at, at + PROBES_AT_ONCE)
            pooled = mm(values_ref[rows, cell : cell + KEYS_AT_ONCE], raw[:, lanes])
            if cell > 0:
                pooled = pooled + fade[:, lanes] * pooled_ref[rows, lanes]
            if cell + KEYS_AT_ONCE == pixels:
                pooled = pooled / total[:, lanes]
            pooled_ref[rows, lanes] = pooled
        old_top, old_total = top, total
    joined = jnp.concatenate(
        [
            pooled_ref[h * head_width : (h + 1) * head_width, h * tokens : (h + 1) * tokens]
            for h in range(HEADS)
        ],
        axis=0,
    ).T
    for at in FETCH_ORDER[9:]:
        copies[at].wait()
    queries = layer_norm(queries + wide_mm(joined, t2i_out_ref[...]), gains_ref[1:2])
    hidden = jnp.maximum(token_mm(queries, mlp_up_ref[...]), 0.0)
    queries = layer_norm(queries + token_mm(hidden, mlp_down_ref[...]), gains_ref[2:3])

    back_k = wide_mm(queries + start, i2t_qkv_ref[:, inner : 2 * inner])
    back_v = wide_mm(queries, i2t_qkv_ref[:, 2 * inner :])
    gaps = by_group(back_k[:slots] - back_k[slots:], inner)
    gaps = wide_mm(gaps, i2t_qkv_ref[:, :inner], mm_t) * (0.5 * head_scale)
    gaps = gaps.astype(bf16)
    middle = 0.5 * (back_v[:slots] + back_v[slots:])
    apart = by_group(0.5 * (back_v[:slots] - back_v[slots:]), inner)
    moves = wide_mm(jnp.concatenate([apart, middle], axis=0), i2t_out_ref[...])
    moves = (moves - jnp.mean(moves, axis=1, keepdims=True)).astype(bf16)
    hyper = wide_mm(jnp.maximum(wide_mm(queries[:slots], hyper_ref[0]), 0.0), hyper_ref[1])
    hyper = hyper.astype(bf16).astype(f32) * gains_ref[3:4]
    hyper = (hyper - jnp.mean(hyper, axis=1, keepdims=True)).astype(bf16)
    apart, middle = moves[: HEADS * slots], moves[HEADS * slots :]
    middle_wide, hyper_wide = middle.astype(f32), hyper.astype(f32)
    consts = jnp.concatenate(
        [
            jnp.sum(middle_wide * middle_wide, axis=1, keepdims=True),
            jnp.sum(middle_wide * hyper_wide, axis=1, keepdims=True),
        ],
        axis=1,
    )
    block = HEADS * SLOT_GROUP
    tall = block + 2 * SLOT_GROUP
    row_slot = lax.rem(lax.broadcasted_iota(jnp.int32, (tall, block), 0), SLOT_GROUP)
    column_slot = lax.rem(lax.broadcasted_iota(jnp.int32, (tall, block), 1), SLOT_GROUP)
    on_cells, on_weights = [], []
    for at in range(0, slots, SLOT_GROUP):
        mine = apart[at * HEADS : (at + SLOT_GROUP) * HEADS]
        mine_twice = (2.0 * mine.astype(f32)).astype(bf16)
        centre_twice = (2.0 * middle_wide[at : at + SLOT_GROUP]).astype(bf16)
        mask = hyper[at : at + SLOT_GROUP]
        on_cells += [mine_twice, centre_twice, mask]
        crossed = mm_t(jnp.concatenate([mine, centre_twice, mask], axis=0), mine)
        on_weights.append(jnp.where(row_slot == column_slot, crossed, 0.0).astype(bf16))
    on_cells.append(jnp.ones((SLOT_GROUP, width), bf16))
    on_cells = jnp.concatenate(on_cells, axis=0)
    on_weights = jnp.concatenate(on_weights, axis=0)
    gaps_ref[...] = gaps
    on_cells_ref[...] = on_cells
    on_weights_ref[...] = on_weights
    consts_ref[...] = consts

    live = counts_ref[0, lax.axis_index("row")]
    weights = cell_weights(gaps, seam_keys_ref[...].astype(bf16))
    _, covers = cell_logits(
        weights, seam_cells_ref[...].astype(bf16), on_cells, on_weights, consts, live
    )
    count = 2 * SEAM * side
    line = lax.broadcasted_iota(jnp.int32, (side, count), 0)
    column = lax.broadcasted_iota(jnp.int32, (side, count), 1)
    near = (column >= line * 2 * SEAM) & (column < (line + 1) * 2 * SEAM)
    ours = lax.rem(lax.broadcasted_iota(jnp.int32, (count, side), 0), 2 * SEAM)
    theirs = lax.broadcasted_iota(jnp.int32, (count, side), 1)
    left = jnp.where(ours < SEAM, SEAM + 1 - (side + ours - theirs), 0)
    right = jnp.where(ours >= SEAM, SEAM + 1 - (theirs + 2 * SEAM - ours), 0)
    lines = jnp.where(near, covers, 0.0)
    scale = 1.0 / (SEAM + 1) ** 2
    to_left = scale * wide_mm(lines, jnp.maximum(left, 0).astype(f32).astype(bf16))
    to_right = scale * wide_mm(lines, jnp.maximum(right, 0).astype(f32).astype(bf16))
    even = lax.rem(lax.axis_index("col"), 2) == 0
    even_ref[...] = jnp.where(even, to_right, to_left)
    odd_ref[...] = jnp.where(even, to_left, to_right)


def image_kernel(
    counts_ref,
    cells_ref,
    keys_ref,
    gaps_ref,
    on_cells_ref,
    on_weights_ref,
    consts_ref,
    logits_ref,
    blended_ref,
    coverage_ref,
    found_ref,
    sems,
):
    pixels, width = cells_ref.shape
    side = math.isqrt(pixels)
    live = counts_ref[0, lax.axis_index("row")]
    gaps, on_cells, on_weights = gaps_ref[...], on_cells_ref[...], on_weights_ref[...]
    consts = consts_ref[...]
    places = [slice(at, at + CELLS_AT_ONCE) for at in range(0, pixels, CELLS_AT_ONCE)]
    weights = cell_weights(gaps, keys_ref[places[0], :])
    copies = []
    for step, place in enumerate(places):
        now = weights
        if step + 1 < len(places):
            weights = cell_weights(gaps, keys_ref[places[step + 1], :])
        logits, covers = cell_logits(now, cells_ref[place, :], on_cells, on_weights, consts, live)
        found_ref[:, place] = logits
        copies.append(
            pltpu.make_async_copy(found_ref.at[:, place], logits_ref.at[:, place], sems.at[step])
        )
        copies[-1].start()
        for at in range(0, CELLS_AT_ONCE, side):
            line = (step * CELLS_AT_ONCE + at) // side
            coverage_ref[line : line + 1, :] = covers[:, at : at + side]
    apart = jnp.abs(
        lax.broadcasted_iota(jnp.int32, (side, side), 0)
        - lax.broadcasted_iota(jnp.int32, (side, side), 1)
    )
    band = jnp.maximum(SEAM + 1 - apart, 0).astype(f32).astype(bf16)
    blended_ref[...] = (1.0 / (SEAM + 1) ** 2) * wide_mm(coverage_ref[...], band)
    for copy in copies:
        copy.wait()


def shards(
    embedding,
    counts,
    points,
    pe_gauss,
    point_embed,
    mask_token,
    sa_qkv,
    sa_out,
    t2i_qkv,
    t2i_out,
    mlp_up,
    mlp_down,
    i2t_qkv,
    i2t_out,
    hyper_w,
    ln_gains,
):
    side = embedding.shape[0]
    width = embedding.shape[2]
    inner = t2i_qkv.shape[1] // 3
    slots = points.shape[3]
    pixels = side * side
    groups = slots // SLOT_GROUP
    tall = (HEADS + 2) * SLOT_GROUP
    whole = pl.BlockSpec(memory_space=pltpu.VMEM)
    scalars = pl.BlockSpec(memory_space=pltpu.SMEM)
    cells = embedding.reshape(pixels, width)
    shape = jax.ShapeDtypeStruct
    params = pltpu.CompilerParams(vmem_limit_bytes=36 << 20)
    far = pl.BlockSpec(memory_space=pltpu.HBM)
    arrays = [
        pltpu.with_memory_space_constraint(one, pltpu.HBM)
        for one in (
            counts,
            points.reshape(2, slots),
            pe_gauss,
            point_embed.reshape(1, width),
            mask_token.reshape(1, width),
            sa_qkv,
            sa_out,
            t2i_qkv,
            t2i_out,
            mlp_up,
            mlp_down,
            i2t_qkv,
            i2t_out,
            hyper_w,
            ln_gains,
            cells,
        )
    ]
    *slot_side, even, odd = pl.pallas_call(
        decode_kernel,
        out_shape=(
            shape((pixels, width), bf16),
            shape((pixels, width), bf16),
            shape((HEADS * slots, width), bf16),
            shape((groups * tall + SLOT_GROUP, width), bf16),
            shape((groups * tall, HEADS * SLOT_GROUP), bf16),
            shape((slots, 2), f32),
            shape((side, side), f32),
            shape((side, side), f32),
        ),
        in_specs=[far] * ARRAYS,
        out_specs=(whole,) * 8,
        scratch_shapes=[pltpu.SMEM(counts.shape, counts.dtype)]
        + [pltpu.VMEM(one.shape, one.dtype) for one in arrays[1:-1]]
        + [
            pltpu.SemaphoreType.DMA((ARRAYS,)),
            pltpu.VMEM((2 * SEAM * side, width), f32),
            pltpu.VMEM((2 * SEAM * side, width), f32),
            pltpu.VMEM((inner, pixels), bf16),
            pltpu.VMEM((inner, 2 * slots * HEADS), f32),
        ],
        compiler_params=params,
        name="decode",
    )(*arrays)
    count = lax.axis_size("col")
    swaps = [
        [pair for i in range(first, count - 1, 2) for pair in ((i, i + 1), (i + 1, i))]
        for first in (0, 1)
    ]
    odd = lax.ppermute(odd, "col", swaps[1])
    even = lax.ppermute(even, "col", swaps[0])
    logits, blended = pl.pallas_call(
        image_kernel,
        out_shape=(shape((slots, pixels), bf16), shape((side, side), f32)),
        in_specs=[scalars] + [whole] * 6,
        out_specs=(pl.BlockSpec(memory_space=pltpu.HBM), whole),
        scratch_shapes=[
            pltpu.VMEM((side, side), f32),
            pltpu.VMEM((slots, pixels), bf16),
            pltpu.SemaphoreType.DMA((pixels // CELLS_AT_ONCE,)),
        ],
        compiler_params=params,
        name="image",
    )(arrays[0], *slot_side)
    return (logits.reshape(1, 1, slots, pixels), blended + even + odd)


def solution(mesh):
    placed = (P("row", "col", None), P("col", None), P("row", "col", None, None)) + (P(),) * 13
    return jax.shard_map(
        shards,
        mesh=mesh,
        in_specs=placed,
        out_specs=(P("row", "col", None, None), P("row", "col")),
        check_vma=False,
    )
```

```python
import functools
import math

import jax
import jax.numpy as jnp
from jax import lax
from jax.experimental import pallas as pl
from jax.experimental.pallas import tpu as pltpu
from jax.sharding import PartitionSpec as P

HEADS = 8
SEAM = 4
IMG = 1024
SLOT_GROUP = 16
KEYS_AT_ONCE = 1024
PROBES_AT_ONCE = 256
FOLD = 64
IN_RANGE = 2.0**96
ARRAYS = 16
FETCH_ORDER = (2, 1, 4, 3, 14, 5, 6, 7, 15, 8, 9, 10, 11, 12, 13, 0)
CELLS_AT_ONCE = 512

norm_eps = 1e-05
bf16 = jnp.bfloat16
f32 = jnp.float32


def mm(left, right):
    return lax.dot_general(left, right, (((1,), (0,)), ((), ())), preferred_element_type=f32)


def mm_t(left, right):
    return lax.dot_general(left, right, (((1,), (1,)), ((), ())), preferred_element_type=f32)


def halves(values):
    high = values.astype(bf16)
    low = (values - high.astype(f32)).astype(bf16)
    return jnp.concatenate([high, low], axis=0)


def wide_mm(values, weight, product=mm):
    rows = values.shape[0]
    both = product(halves(values), weight)
    return both[:rows] + both[rows:]


def token_mm(values, weight):
    return mm(values.astype(bf16), weight)


def layer_norm(values, gain):
    centred = values - jnp.mean(values, axis=-1, keepdims=True)
    spread = jnp.mean(centred * centred, axis=-1, keepdims=True)
    return centred * lax.rsqrt(spread + norm_eps) * gain


def sin_turns(turns):
    part = turns - jnp.floor(turns + 0.5)
    size = 0.25 - jnp.abs(jnp.abs(part) - 0.25)
    angle = (2.0 * math.pi) * jnp.where(part < 0.0, -size, size)
    square = angle * angle
    total = jnp.full_like(angle, -1.0 / math.factorial(11))
    for order in (9, 7, 5, 3, 1):
        sign = 1.0 if order % 4 == 1 else -1.0
        total = total * square + sign / math.factorial(order)
    return total * angle


def fold_rows(values, join):
    total = values[:FOLD]
    for at in range(FOLD, values.shape[0], FOLD):
        total = join(total, values[at : at + FOLD])
    rows = FOLD
    while rows > 1:
        rows //= 2
        total = join(total[:rows], total[rows:])
    return total


def by_head(rows, inner_width):
    head_width = inner_width // HEADS
    lane = lax.broadcasted_iota(jnp.int32, rows.shape, 1)
    return jnp.concatenate(
        [
            jnp.where((lane >= h * head_width) & (lane < (h + 1) * head_width), rows, 0.0)
            for h in range(HEADS)
        ],
        axis=0,
    )


def by_group(rows, inner_width):
    return jnp.concatenate(
        [
            by_head(rows[at : at + SLOT_GROUP], inner_width)
            for at in range(0, rows.shape[0], SLOT_GROUP)
        ],
        axis=0,
    )


def group_ones(width, group):
    row = lax.broadcasted_iota(jnp.int32, (width, width), 0)
    column = lax.broadcasted_iota(jnp.int32, (width, width), 1)
    first = row - lax.rem(row, group)
    return jnp.where((column >= first) & (column < first + group), 1.0, 0.0).astype(bf16)


def cell_weights(gaps, keys):
    return jnp.tanh(mm_t(gaps, keys)).astype(bf16)


def cell_logits(weights, cells, on_cells, on_weights, consts, live):
    count, width = cells.shape
    slots = consts.shape[0]
    block = HEADS * SLOT_GROUP
    tall = block + 2 * SLOT_GROUP
    flat = mm_t(on_cells, cells)
    wide = cells.astype(f32)
    norms = jnp.sum(wide * wide, axis=1, keepdims=True)
    lanes = 128
    same = lax.broadcasted_iota(jnp.int32, (lanes, lanes), 0) == lax.broadcasted_iota(
        jnp.int32, (lanes, lanes), 1
    )
    norms = jnp.concatenate(
        [
            jnp.sum(jnp.where(same, norms[at : at + lanes], 0.0), axis=0, keepdims=True)
            for at in range(0, count, lanes)
        ],
        axis=1,
    )
    total = flat[slots // SLOT_GROUP * tall :][:SLOT_GROUP]
    norms = norms - total * total * (1.0 / width)
    logits, covers = [], []
    for at in range(0, slots, SLOT_GROUP):
        group = at // SLOT_GROUP
        mine = weights[group * block : (group + 1) * block]
        both = flat[group * tall : (group + 1) * tall] + mm(
            on_weights[group * tall : (group + 1) * tall], mine
        )
        square = norms + both[block : block + SLOT_GROUP] + consts[at : at + SLOT_GROUP, 0:1]
        for h in range(HEADS):
            part = slice(h * SLOT_GROUP, (h + 1) * SLOT_GROUP)
            square = square + mine[part].astype(f32) * both[part]
        dots = both[block + SLOT_GROUP :] + consts[at : at + SLOT_GROUP, 1:2]
        kept = at + lax.broadcasted_iota(jnp.int32, (SLOT_GROUP, count), 0) < live
        found = dots * lax.rsqrt(jnp.maximum(square, 0.0) + width * norm_eps)
        found = jnp.where(kept, found, 0.0).astype(bf16)
        logits.append(found)
        covers.append(jnp.where(kept, 0.5 * jnp.tanh(0.5 * found.astype(f32)) + 0.5, 0.0))
    return jnp.concatenate(logits, axis=0), jnp.sum(sum(covers), axis=0, keepdims=True)


def decode_kernel(*refs):
    far, refs = refs[:ARRAYS], refs[ARRAYS:]
    (cells_ref, *slot_side), refs = refs[:8], refs[8:]
    near, (sems, *scratch) = refs[: ARRAYS - 1], refs[ARRAYS - 1 :]
    near = [*near, cells_ref]
    copies = [pltpu.make_async_copy(*pair, sems.at[at]) for at, pair in enumerate(zip(far, near))]
    for at in FETCH_ORDER:
        copies[at].start()
    decode(copies, *near, *slot_side, *scratch)


def decode(
    copies,
    counts_ref,
    points_ref,
    gauss_ref,
    point_embed_ref,
    mask_token_ref,
    sa_qkv_ref,
    sa_out_ref,
    t2i_qkv_ref,
    t2i_out_ref,
    mlp_up_ref,
    mlp_down_ref,
    i2t_qkv_ref,
    i2t_out_ref,
    hyper_ref,
    gains_ref,
    cells_ref,
    keys_ref,
    gaps_ref,
    on_cells_ref,
    on_weights_ref,
    consts_ref,
    even_ref,
    odd_ref,
    seam_cells_ref,
    seam_keys_ref,
    values_ref,
    pooled_ref,
):
    pixels, width = cells_ref.shape
    side = math.isqrt(pixels)
    slots = points_ref.shape[1]
    inner = t2i_qkv_ref.shape[1] // 3
    head_width = inner // HEADS
    half = width // 2
    for at in FETCH_ORDER[:5]:
        copies[at].wait()

    gauss = gauss_ref[...]
    steps = lax.broadcasted_iota(jnp.int32, (side, half), 0).astype(f32)
    steps = (2.0 * (steps + 0.5)) / side - 1.0
    spots = jnp.clip(points_ref[...], 0, IMG - 1).astype(f32)
    spots = 2.0 * ((spots + 0.5) / IMG) - 1.0
    same = lax.broadcasted_iota(jnp.int32, (slots, slots), 0) == lax.broadcasted_iota(
        jnp.int32, (slots, slots), 1
    )
    spot_x = jnp.sum(jnp.where(same, spots[0:1], 0.0), axis=1, keepdims=True)
    spot_y = jnp.sum(jnp.where(same, spots[1:2], 0.0), axis=1, keepdims=True)
    turns = jnp.concatenate(
        [steps * gauss[0:1], steps * gauss[1:2], spot_x * gauss[0:1] + spot_y * gauss[1:2]], axis=0
    )
    sines = sin_turns(turns)
    cosines = sin_turns(turns + 0.25)
    prompt = jnp.concatenate([sines[2 * side :], cosines[2 * side :]], axis=1)

    start = jnp.concatenate(
        [
            jnp.broadcast_to(mask_token_ref[...], (slots, width)),
            prompt + point_embed_ref[...],
        ],
        axis=0,
    )
    for at in FETCH_ORDER[5:8]:
        copies[at].wait()
    qkv = wide_mm(start, sa_qkv_ref[...])
    query, key, value = qkv[:, :width], qkv[:, width : 2 * width], qkv[:, 2 * width :]
    key_gap = key[:slots] - key[slots:]
    value_gap = value[:slots] - value[slots:]
    scores = wide_mm(
        query * jnp.concatenate([key_gap, key_gap], axis=0), group_ones(width, width // HEADS)
    )
    first = 0.5 * jnp.tanh((0.5 / math.sqrt(width // HEADS)) * scores) + 0.5
    attended = jnp.concatenate([value[slots:]] * 2, axis=0) + first * jnp.concatenate(
        [value_gap, value_gap], axis=0
    )
    queries = layer_norm(wide_mm(attended, sa_out_ref[...]), gains_ref[0:1])
    head_scale = 1.0 / math.sqrt(head_width)
    cross_q = wide_mm(queries + start, t2i_qkv_ref[:, :inner])
    cross_q = by_head(cross_q, inner).astype(bf16)
    probes = mm_t(cross_q, t2i_qkv_ref[:, inner : 2 * inner]) * (head_scale * math.log2(math.e))
    probes = probes.astype(bf16)

    copies[FETCH_ORDER[8]].wait()
    sin_x, cos_x = sines[:side], cosines[:side]
    left_half = lax.broadcasted_iota(jnp.int32, (2 * SEAM, width), 0) < SEAM
    for line in range(side):
        sin_y, cos_y = sines[side + line : side + line + 1], cosines[side + line : side + line + 1]
        place = slice(line * side, (line + 1) * side)
        encoding = jnp.concatenate(
            [sin_x * cos_y + cos_x * sin_y, cos_x * cos_y - sin_x * sin_y], axis=1
        )
        own = cells_ref[place, :].astype(f32)
        keys = own + encoding
        keys_ref[place, :] = keys.astype(bf16)
        seam = slice(line * 2 * SEAM, (line + 1) * 2 * SEAM)
        seam_cells_ref[seam, :] = jnp.where(left_half, own[: 2 * SEAM], own[side - 2 * SEAM :])
        seam_keys_ref[seam, :] = jnp.where(left_half, keys[: 2 * SEAM], keys[side - 2 * SEAM :])

    values_ref[...] = mm_t(
        t2i_qkv_ref[:, 2 * inner :].astype(f32).T.astype(bf16), cells_ref[...]
    ).astype(bf16)
    tokens = start.shape[0]
    ones = jnp.ones((head_width, KEYS_AT_ONCE), bf16)
    tiles = []
    for at in range(0, HEADS * tokens, PROBES_AT_ONCE):
        rows = slice(
            at // tokens * head_width, ((at + PROBES_AT_ONCE - 1) // tokens + 1) * head_width
        )
        tiles.append((rows, slice(at, at + PROBES_AT_ONCE)))

    def raw_scores(cell):
        return mm_t(keys_ref[cell : cell + KEYS_AT_ONCE, :], probes)

    def pool(cell, rows, share):
        near = values_ref[rows, cell : cell + KEYS_AT_ONCE]
        return mm(jnp.concatenate([near, ones], axis=0), share)

    sums = [0.0] * len(tiles)
    ahead = raw_scores(0)
    for cell in range(0, pixels, KEYS_AT_ONCE):
        raw = ahead
        if cell + KEYS_AT_ONCE < pixels:
            ahead = raw_scores(cell + KEYS_AT_ONCE)
        share = jnp.exp2(raw).astype(bf16)
        sums = [
            total + pool(cell, rows, share[:, lanes]) for total, (rows, lanes) in zip(sums, tiles)
        ]
    inside = []
    for total, (rows, lanes) in zip(sums, tiles):
        whole = total[-head_width : -head_width + 1]
        inside.append((whole >= 1.0 / IN_RANGE) & (whole <= IN_RANGE))
        pooled_ref[rows, lanes] = total[:-head_width] / whole
    inside = jnp.min(jnp.concatenate(inside, axis=1).astype(f32))

    @pl.when(inside < 0.5)
    def _():
        sums = [0.0] * len(tiles)
        for cell in range(0, pixels, KEYS_AT_ONCE):
            raw = raw_scores(cell)
            top = fold_rows(raw, jnp.maximum)
            if cell > 0:
                top = jnp.maximum(top, old_top)
                fade = jnp.exp2(old_top - top)
                sums = [total * fade[:, lanes] for total, (rows, lanes) in zip(sums, tiles)]
            old_top = top
            share = jnp.exp2(raw - top).astype(bf16)
            sums = [
                total + pool(cell, rows, share[:, lanes])
                for total, (rows, lanes) in zip(sums, tiles)
            ]
        for total, (rows, lanes) in zip(sums, tiles):
            pooled_ref[rows, lanes] = total[:-head_width] / total[-head_width : -head_width + 1]

    joined = jnp.concatenate(
        [
            pooled_ref[h * head_width : (h + 1) * head_width, h * tokens : (h + 1) * tokens]
            for h in range(HEADS)
        ],
        axis=0,
    ).T
    for at in FETCH_ORDER[9:]:
        copies[at].wait()
    queries = layer_norm(queries + wide_mm(joined, t2i_out_ref[...]), gains_ref[1:2])
    hidden = jnp.maximum(token_mm(queries, mlp_up_ref[...]), 0.0)
    queries = layer_norm(queries + token_mm(hidden, mlp_down_ref[...]), gains_ref[2:3])

    back_k = wide_mm(queries + start, i2t_qkv_ref[:, inner : 2 * inner])
    back_v = wide_mm(queries, i2t_qkv_ref[:, 2 * inner :])
    gaps = by_group(back_k[:slots] - back_k[slots:], inner)
    gaps = wide_mm(gaps, i2t_qkv_ref[:, :inner], mm_t) * (0.5 * head_scale)
    gaps = gaps.astype(bf16)
    middle = 0.5 * (back_v[:slots] + back_v[slots:])
    apart = by_group(0.5 * (back_v[:slots] - back_v[slots:]), inner)
    moves = wide_mm(jnp.concatenate([apart, middle], axis=0), i2t_out_ref[...])
    moves = (moves - jnp.mean(moves, axis=1, keepdims=True)).astype(bf16)
    hyper = wide_mm(jnp.maximum(wide_mm(queries[:slots], hyper_ref[0]), 0.0), hyper_ref[1])
    hyper = hyper.astype(bf16).astype(f32) * gains_ref[3:4]
    hyper = (hyper - jnp.mean(hyper, axis=1, keepdims=True)).astype(bf16)
    apart, middle = moves[: HEADS * slots], moves[HEADS * slots :]
    middle_wide, hyper_wide = middle.astype(f32), hyper.astype(f32)
    consts = jnp.concatenate(
        [
            jnp.sum(middle_wide * middle_wide, axis=1, keepdims=True),
            jnp.sum(middle_wide * hyper_wide, axis=1, keepdims=True),
        ],
        axis=1,
    )
    block = HEADS * SLOT_GROUP
    tall = block + 2 * SLOT_GROUP
    row_slot = lax.rem(lax.broadcasted_iota(jnp.int32, (tall, block), 0), SLOT_GROUP)
    column_slot = lax.rem(lax.broadcasted_iota(jnp.int32, (tall, block), 1), SLOT_GROUP)
    on_cells, on_weights = [], []
    for at in range(0, slots, SLOT_GROUP):
        mine = apart[at * HEADS : (at + SLOT_GROUP) * HEADS]
        mine_twice = (2.0 * mine.astype(f32)).astype(bf16)
        centre_twice = (2.0 * middle_wide[at : at + SLOT_GROUP]).astype(bf16)
        mask = hyper[at : at + SLOT_GROUP]
        on_cells += [mine_twice, centre_twice, mask]
        crossed = mm_t(jnp.concatenate([mine, centre_twice, mask], axis=0), mine)
        on_weights.append(jnp.where(row_slot == column_slot, crossed, 0.0).astype(bf16))
    on_cells.append(jnp.ones((SLOT_GROUP, width), bf16))
    on_cells = jnp.concatenate(on_cells, axis=0)
    on_weights = jnp.concatenate(on_weights, axis=0)
    gaps_ref[...] = gaps
    on_cells_ref[...] = on_cells
    on_weights_ref[...] = on_weights
    consts_ref[...] = consts

    live = counts_ref[0, lax.axis_index("row")]
    weights = cell_weights(gaps, seam_keys_ref[...].astype(bf16))
    _, covers = cell_logits(
        weights, seam_cells_ref[...].astype(bf16), on_cells, on_weights, consts, live
    )
    count = 2 * SEAM * side
    line = lax.broadcasted_iota(jnp.int32, (side, count), 0)
    column = lax.broadcasted_iota(jnp.int32, (side, count), 1)
    near = (column >= line * 2 * SEAM) & (column < (line + 1) * 2 * SEAM)
    ours = lax.rem(lax.broadcasted_iota(jnp.int32, (count, side), 0), 2 * SEAM)
    theirs = lax.broadcasted_iota(jnp.int32, (count, side), 1)
    left = jnp.where(ours < SEAM, SEAM + 1 - (side + ours - theirs), 0)
    right = jnp.where(ours >= SEAM, SEAM + 1 - (theirs + 2 * SEAM - ours), 0)
    lines = jnp.where(near, covers, 0.0)
    scale = 1.0 / (SEAM + 1) ** 2
    to_left = scale * wide_mm(lines, jnp.maximum(left, 0).astype(f32).astype(bf16))
    to_right = scale * wide_mm(lines, jnp.maximum(right, 0).astype(f32).astype(bf16))
    column = lax.axis_index("col")
    to_left = jnp.where(column > 0, to_left, 0.0)
    to_right = jnp.where(column < lax.axis_size("col") - 1, to_right, 0.0)
    even = lax.rem(column, 2) == 0
    even_ref[...] = jnp.where(even, to_right, to_left)
    odd_ref[...] = jnp.where(even, to_left, to_right)


def image_kernel(
    counts_ref,
    cells_ref,
    keys_ref,
    gaps_ref,
    on_cells_ref,
    on_weights_ref,
    consts_ref,
    logits_ref,
    blended_ref,
    coverage_ref,
    found_ref,
    sems,
):
    pixels, width = cells_ref.shape
    side = math.isqrt(pixels)
    live = counts_ref[0, lax.axis_index("row")]
    gaps, on_cells, on_weights = gaps_ref[...], on_cells_ref[...], on_weights_ref[...]
    consts = consts_ref[...]
    places = [slice(at, at + CELLS_AT_ONCE) for at in range(0, pixels, CELLS_AT_ONCE)]
    weights = cell_weights(gaps, keys_ref[places[0], :])
    copies = []
    for step, place in enumerate(places):
        now = weights
        if step + 1 < len(places):
            weights = cell_weights(gaps, keys_ref[places[step + 1], :])
        logits, covers = cell_logits(now, cells_ref[place, :], on_cells, on_weights, consts, live)
        found_ref[:, place] = logits
        copies.append(
            pltpu.make_async_copy(found_ref.at[:, place], logits_ref.at[:, place], sems.at[step])
        )
        copies[-1].start()
        for at in range(0, CELLS_AT_ONCE, side):
            line = (step * CELLS_AT_ONCE + at) // side
            coverage_ref[line : line + 1, :] = covers[:, at : at + side]
    apart = jnp.abs(
        lax.broadcasted_iota(jnp.int32, (side, side), 0)
        - lax.broadcasted_iota(jnp.int32, (side, side), 1)
    )
    band = jnp.maximum(SEAM + 1 - apart, 0).astype(f32).astype(bf16)
    blended_ref[...] = (1.0 / (SEAM + 1) ** 2) * wide_mm(coverage_ref[...], band)
    for copy in copies:
        copy.wait()


def shards(
    embedding,
    counts,
    points,
    pe_gauss,
    point_embed,
    mask_token,
    sa_qkv,
    sa_out,
    t2i_qkv,
    t2i_out,
    mlp_up,
    mlp_down,
    i2t_qkv,
    i2t_out,
    hyper_w,
    ln_gains,
):
    side = embedding.shape[0]
    width = embedding.shape[2]
    inner = t2i_qkv.shape[1] // 3
    slots = points.shape[3]
    pixels = side * side
    groups = slots // SLOT_GROUP
    tall = (HEADS + 2) * SLOT_GROUP
    whole = pl.BlockSpec(memory_space=pltpu.VMEM)
    scalars = pl.BlockSpec(memory_space=pltpu.SMEM)
    cells = embedding.reshape(pixels, width)
    shape = jax.ShapeDtypeStruct
    params = pltpu.CompilerParams(vmem_limit_bytes=36 << 20)
    far = pl.BlockSpec(memory_space=pltpu.HBM)
    arrays = [
        pltpu.with_memory_space_constraint(one, pltpu.HBM)
        for one in (
            counts,
            points.reshape(2, slots),
            pe_gauss,
            point_embed.reshape(1, width),
            mask_token.reshape(1, width),
            sa_qkv,
            sa_out,
            t2i_qkv,
            t2i_out,
            mlp_up,
            mlp_down,
            i2t_qkv,
            i2t_out,
            hyper_w,
            ln_gains,
            cells,
        )
    ]
    *slot_side, even, odd = pl.pallas_call(
        decode_kernel,
        out_shape=(
            shape((pixels, width), bf16),
            shape((pixels, width), bf16),
            shape((HEADS * slots, width), bf16),
            shape((groups * tall + SLOT_GROUP, width), bf16),
            shape((groups * tall, HEADS * SLOT_GROUP), bf16),
            shape((slots, 2), f32),
            shape((side, side), f32),
            shape((side, side), f32),
        ),
        in_specs=[far] * ARRAYS,
        out_specs=(whole,) * 8,
        scratch_shapes=[pltpu.SMEM(counts.shape, counts.dtype)]
        + [pltpu.VMEM(one.shape, one.dtype) for one in arrays[1:-1]]
        + [
            pltpu.SemaphoreType.DMA((ARRAYS,)),
            pltpu.VMEM((2 * SEAM * side, width), f32),
            pltpu.VMEM((2 * SEAM * side, width), f32),
            pltpu.VMEM((inner, pixels), bf16),
            pltpu.VMEM((inner, 2 * slots * HEADS), f32),
        ],
        compiler_params=params,
        name="decode",
    )(*arrays)
    count = lax.axis_size("col")
    rows = lax.axis_size("row")
    swaps = []
    for first in (0, 1):
        pairs = []
        for row in range(rows):
            for column in range(count):
                other = column + 1 if column % 2 == first else column - 1
                if 0 <= other < count:
                    partner = row * count + other
                else:
                    partner = min(row ^ 1, rows - 1) * count + column
                pairs.append((row * count + column, partner))
        swaps.append(pairs)
    odd = lax.ppermute(odd, ("row", "col"), swaps[1])
    even = lax.ppermute(even, ("row", "col"), swaps[0])
    logits, blended = pl.pallas_call(
        image_kernel,
        out_shape=(shape((slots, pixels), bf16), shape((side, side), f32)),
        in_specs=[scalars] + [whole] * 6,
        out_specs=(pl.BlockSpec(memory_space=pltpu.HBM), whole),
        scratch_shapes=[
            pltpu.VMEM((side, side), f32),
            pltpu.VMEM((slots, pixels), bf16),
            pltpu.SemaphoreType.DMA((pixels // CELLS_AT_ONCE,)),
        ],
        compiler_params=params,
        name="image",
    )(arrays[0], *slot_side)
    return (logits.reshape(1, 1, slots, pixels), blended + even + odd)


def solution(mesh):
    placed = (P("row", "col", None), P("col", None), P("row", "col", None, None)) + (P(),) * 13
    return jax.shard_map(
        shards,
        mesh=mesh,
        in_specs=placed,
        out_specs=(P("row", "col", None, None), P("row", "col")),
        check_vma=False,
    )
```

```python
import functools
import math

import jax
import jax.numpy as jnp
from jax import lax
from jax.experimental import pallas as pl
from jax.experimental.pallas import tpu as pltpu
from jax.sharding import PartitionSpec as P

HEADS = 8
SEAM = 4
IMG = 1024
SLOT_GROUP = 16
KEYS_AT_ONCE = 1024
PROBES_AT_ONCE = 256
FOLD = 64
IN_RANGE = 2.0**96
ARRAYS = 16
FETCH_ORDER = (2, 1, 4, 3, 14, 5, 6, 7, 15, 8, 9, 10, 11, 12, 13, 0)
CELLS_AT_ONCE = 512

norm_eps = 1e-05
bf16 = jnp.bfloat16
f32 = jnp.float32


def mm(left, right):
    return lax.dot_general(left, right, (((1,), (0,)), ((), ())), preferred_element_type=f32)


def mm_t(left, right):
    return lax.dot_general(left, right, (((1,), (1,)), ((), ())), preferred_element_type=f32)


def halves(values):
    high = values.astype(bf16)
    low = (values - high.astype(f32)).astype(bf16)
    return jnp.concatenate([high, low], axis=0)


def wide_mm(values, weight, product=mm):
    rows = values.shape[0]
    both = product(halves(values), weight)
    return both[:rows] + both[rows:]


def token_mm(values, weight):
    return mm(values.astype(bf16), weight)


def layer_norm(values, gain):
    centred = values - jnp.mean(values, axis=-1, keepdims=True)
    spread = jnp.mean(centred * centred, axis=-1, keepdims=True)
    return centred * lax.rsqrt(spread + norm_eps) * gain


def sin_turns(turns):
    part = turns - jnp.floor(turns + 0.5)
    size = 0.25 - jnp.abs(jnp.abs(part) - 0.25)
    angle = (2.0 * math.pi) * jnp.where(part < 0.0, -size, size)
    square = angle * angle
    total = jnp.full_like(angle, -1.0 / math.factorial(11))
    for order in (9, 7, 5, 3, 1):
        sign = 1.0 if order % 4 == 1 else -1.0
        total = total * square + sign / math.factorial(order)
    return total * angle


def fold_rows(values, join):
    total = values[:FOLD]
    for at in range(FOLD, values.shape[0], FOLD):
        total = join(total, values[at : at + FOLD])
    rows = FOLD
    while rows > 1:
        rows //= 2
        total = join(total[:rows], total[rows:])
    return total


def by_head(rows, inner_width):
    head_width = inner_width // HEADS
    lane = lax.broadcasted_iota(jnp.int32, rows.shape, 1)
    return jnp.concatenate(
        [
            jnp.where((lane >= h * head_width) & (lane < (h + 1) * head_width), rows, 0.0)
            for h in range(HEADS)
        ],
        axis=0,
    )


def by_group(rows, inner_width):
    return jnp.concatenate(
        [
            by_head(rows[at : at + SLOT_GROUP], inner_width)
            for at in range(0, rows.shape[0], SLOT_GROUP)
        ],
        axis=0,
    )


def group_ones(width, group):
    row = lax.broadcasted_iota(jnp.int32, (width, width), 0)
    column = lax.broadcasted_iota(jnp.int32, (width, width), 1)
    first = row - lax.rem(row, group)
    return jnp.where((column >= first) & (column < first + group), 1.0, 0.0).astype(bf16)


def cell_weights(gaps, keys, on_cells, cells):
    slots = gaps.shape[0] // HEADS
    flat = mm_t(on_cells, cells)
    weights = jnp.tanh(mm_t(gaps, keys)).astype(bf16)
    return flat[:-slots].astype(bf16), weights, flat[-slots:]


def cell_logits(found, cells, on_weights, consts, live):
    folds, weights, products = found
    count, width = cells.shape
    slots = consts.shape[0]
    block = HEADS * SLOT_GROUP
    tall = block + 2 * SLOT_GROUP
    wide = cells.astype(f32)
    wide = wide - jnp.mean(wide, axis=1, keepdims=True)
    norms = jnp.sum(wide * wide, axis=1, keepdims=True)
    lanes = 128
    same = lax.broadcasted_iota(jnp.int32, (lanes, lanes), 0) == lax.broadcasted_iota(
        jnp.int32, (lanes, lanes), 1
    )
    norms = jnp.concatenate(
        [
            jnp.sum(jnp.where(same, norms[at : at + lanes], 0.0), axis=0, keepdims=True)
            for at in range(0, count, lanes)
        ],
        axis=1,
    )
    logits, covers = [], []
    for at in range(0, slots, SLOT_GROUP):
        group = at // SLOT_GROUP
        mine = weights[group * block : (group + 1) * block]
        both = mm(
            on_weights[group * tall : (group + 1) * tall], jnp.concatenate([folds, mine], axis=0)
        )
        square = norms + both[block : block + SLOT_GROUP] + consts[at : at + SLOT_GROUP, 0:1]
        for h in range(HEADS):
            part = slice(h * SLOT_GROUP, (h + 1) * SLOT_GROUP)
            square = square + mine[part].astype(f32) * both[part]
        dots = both[block + SLOT_GROUP :] + products[at : at + SLOT_GROUP]
        dots = dots + consts[at : at + SLOT_GROUP, 1:2]
        kept = at + lax.broadcasted_iota(jnp.int32, (SLOT_GROUP, count), 0) < live
        found = dots * lax.rsqrt(jnp.maximum(square, 0.0) + width * norm_eps)
        found = jnp.where(kept, found, 0.0).astype(bf16)
        logits.append(found)
        covers.append(jnp.where(kept, 0.5 * jnp.tanh(0.5 * found.astype(f32)) + 0.5, 0.0))
    return jnp.concatenate(logits, axis=0), jnp.sum(sum(covers), axis=0, keepdims=True)


def decode_kernel(*refs):
    far, refs = refs[:ARRAYS], refs[ARRAYS:]
    (cells_ref, *slot_side), refs = refs[:8], refs[8:]
    near, (sems, *scratch) = refs[: ARRAYS - 1], refs[ARRAYS - 1 :]
    near = [*near, cells_ref]
    copies = [pltpu.make_async_copy(*pair, sems.at[at]) for at, pair in enumerate(zip(far, near))]
    for at in FETCH_ORDER:
        copies[at].start()
    decode(copies, *near, *slot_side, *scratch)


def decode(
    copies,
    counts_ref,
    points_ref,
    gauss_ref,
    point_embed_ref,
    mask_token_ref,
    sa_qkv_ref,
    sa_out_ref,
    t2i_qkv_ref,
    t2i_out_ref,
    mlp_up_ref,
    mlp_down_ref,
    i2t_qkv_ref,
    i2t_out_ref,
    hyper_ref,
    gains_ref,
    cells_ref,
    keys_ref,
    gaps_ref,
    on_cells_ref,
    on_weights_ref,
    consts_ref,
    even_ref,
    odd_ref,
    seam_cells_ref,
    seam_keys_ref,
    values_ref,
    pooled_ref,
):
    pixels, width = cells_ref.shape
    side = math.isqrt(pixels)
    slots = points_ref.shape[1]
    inner = t2i_qkv_ref.shape[1] // 3
    head_width = inner // HEADS
    half = width // 2
    for at in FETCH_ORDER[:5]:
        copies[at].wait()

    gauss = gauss_ref[...]
    steps = lax.broadcasted_iota(jnp.int32, (side, half), 0).astype(f32)
    steps = (2.0 * (steps + 0.5)) / side - 1.0
    spots = jnp.clip(points_ref[...], 0, IMG - 1).astype(f32)
    spots = 2.0 * ((spots + 0.5) / IMG) - 1.0
    same = lax.broadcasted_iota(jnp.int32, (slots, slots), 0) == lax.broadcasted_iota(
        jnp.int32, (slots, slots), 1
    )
    spot_x = jnp.sum(jnp.where(same, spots[0:1], 0.0), axis=1, keepdims=True)
    spot_y = jnp.sum(jnp.where(same, spots[1:2], 0.0), axis=1, keepdims=True)
    turns = jnp.concatenate(
        [steps * gauss[0:1], steps * gauss[1:2], spot_x * gauss[0:1] + spot_y * gauss[1:2]], axis=0
    )
    sines = sin_turns(turns)
    cosines = sin_turns(turns + 0.25)
    prompt = jnp.concatenate([sines[2 * side :], cosines[2 * side :]], axis=1)

    start = jnp.concatenate(
        [
            jnp.broadcast_to(mask_token_ref[...], (slots, width)),
            prompt + point_embed_ref[...],
        ],
        axis=0,
    )
    for at in FETCH_ORDER[5:8]:
        copies[at].wait()
    qkv = wide_mm(start, sa_qkv_ref[...])
    query, key, value = qkv[:, :width], qkv[:, width : 2 * width], qkv[:, 2 * width :]
    key_gap = key[:slots] - key[slots:]
    value_gap = value[:slots] - value[slots:]
    scores = wide_mm(
        query * jnp.concatenate([key_gap, key_gap], axis=0), group_ones(width, width // HEADS)
    )
    first = 0.5 * jnp.tanh((0.5 / math.sqrt(width // HEADS)) * scores) + 0.5
    attended = jnp.concatenate([value[slots:]] * 2, axis=0) + first * jnp.concatenate(
        [value_gap, value_gap], axis=0
    )
    queries = layer_norm(wide_mm(attended, sa_out_ref[...]), gains_ref[0:1])
    head_scale = 1.0 / math.sqrt(head_width)
    cross_q = wide_mm(queries + start, t2i_qkv_ref[:, :inner])
    cross_q = by_head(cross_q, inner).astype(bf16)
    probes = mm_t(cross_q, t2i_qkv_ref[:, inner : 2 * inner]) * (head_scale * math.log2(math.e))
    probes = probes.astype(bf16)

    copies[FETCH_ORDER[8]].wait()
    sin_x, cos_x = sines[:side], cosines[:side]
    left_half = lax.broadcasted_iota(jnp.int32, (2 * SEAM, width), 0) < SEAM
    for line in range(side):
        sin_y, cos_y = sines[side + line : side + line + 1], cosines[side + line : side + line + 1]
        place = slice(line * side, (line + 1) * side)
        encoding = jnp.concatenate(
            [sin_x * cos_y + cos_x * sin_y, cos_x * cos_y - sin_x * sin_y], axis=1
        )
        own = cells_ref[place, :].astype(f32)
        keys = own + encoding
        keys_ref[place, :] = keys.astype(bf16)
        seam = slice(line * 2 * SEAM, (line + 1) * 2 * SEAM)
        seam_cells_ref[seam, :] = jnp.where(left_half, own[: 2 * SEAM], own[side - 2 * SEAM :])
        seam_keys_ref[seam, :] = jnp.where(left_half, keys[: 2 * SEAM], keys[side - 2 * SEAM :])

    values_ref[...] = mm_t(
        t2i_qkv_ref[:, 2 * inner :].astype(f32).T.astype(bf16), cells_ref[...]
    ).astype(bf16)
    tokens = start.shape[0]
    ones = jnp.ones((head_width, KEYS_AT_ONCE), bf16)
    tiles = []
    for at in range(0, HEADS * tokens, PROBES_AT_ONCE):
        rows = slice(
            at // tokens * head_width, ((at + PROBES_AT_ONCE - 1) // tokens + 1) * head_width
        )
        tiles.append((rows, slice(at, at + PROBES_AT_ONCE)))

    def raw_scores(cell):
        return mm_t(keys_ref[cell : cell + KEYS_AT_ONCE, :], probes)

    def pool(cell, rows, share):
        near = values_ref[rows, cell : cell + KEYS_AT_ONCE]
        return mm(jnp.concatenate([near, ones], axis=0), share)

    sums = [0.0] * len(tiles)
    ahead = raw_scores(0)
    for cell in range(0, pixels, KEYS_AT_ONCE):
        raw = ahead
        if cell + KEYS_AT_ONCE < pixels:
            ahead = raw_scores(cell + KEYS_AT_ONCE)
        share = jnp.exp2(raw).astype(bf16)
        sums = [
            total + pool(cell, rows, share[:, lanes]) for total, (rows, lanes) in zip(sums, tiles)
        ]
    inside = []
    for total, (rows, lanes) in zip(sums, tiles):
        whole = total[-head_width : -head_width + 1]
        inside.append((whole >= 1.0 / IN_RANGE) & (whole <= IN_RANGE))
        pooled_ref[rows, lanes] = total[:-head_width] / whole
    inside = jnp.min(jnp.concatenate(inside, axis=1).astype(f32))

    @pl.when(inside < 0.5)
    def _():
        sums = [0.0] * len(tiles)
        for cell in range(0, pixels, KEYS_AT_ONCE):
            raw = raw_scores(cell)
            top = fold_rows(raw, jnp.maximum)
            if cell > 0:
                top = jnp.maximum(top, old_top)
                fade = jnp.exp2(old_top - top)
                sums = [total * fade[:, lanes] for total, (rows, lanes) in zip(sums, tiles)]
            old_top = top
            share = jnp.exp2(raw - top).astype(bf16)
            sums = [
                total + pool(cell, rows, share[:, lanes])
                for total, (rows, lanes) in zip(sums, tiles)
            ]
        for total, (rows, lanes) in zip(sums, tiles):
            pooled_ref[rows, lanes] = total[:-head_width] / total[-head_width : -head_width + 1]

    joined = jnp.concatenate(
        [
            pooled_ref[h * head_width : (h + 1) * head_width, h * tokens : (h + 1) * tokens]
            for h in range(HEADS)
        ],
        axis=0,
    ).T
    for at in FETCH_ORDER[9:]:
        copies[at].wait()
    queries = layer_norm(queries + wide_mm(joined, t2i_out_ref[...]), gains_ref[1:2])
    hidden = jnp.maximum(token_mm(queries, mlp_up_ref[...]), 0.0)
    queries = layer_norm(queries + token_mm(hidden, mlp_down_ref[...]), gains_ref[2:3])

    back_k = wide_mm(queries + start, i2t_qkv_ref[:, inner : 2 * inner])
    back_v = wide_mm(queries, i2t_qkv_ref[:, 2 * inner :])
    gaps = by_group(back_k[:slots] - back_k[slots:], inner)
    gaps = wide_mm(gaps, i2t_qkv_ref[:, :inner], mm_t) * (0.5 * head_scale)
    gaps = gaps.astype(bf16)
    middle = 0.5 * (back_v[:slots] + back_v[slots:])
    apart = by_group(0.5 * (back_v[:slots] - back_v[slots:]), inner)
    twice = (2.0 * jnp.concatenate([apart, middle], axis=0)).astype(bf16)
    out_wide = i2t_out_ref[...].astype(f32)
    out_centred = (out_wide - jnp.mean(out_wide, axis=1, keepdims=True)).astype(bf16)
    moves = wide_mm(jnp.concatenate([apart, middle], axis=0), i2t_out_ref[...])
    moves = (moves - jnp.mean(moves, axis=1, keepdims=True)).astype(bf16)
    hyper = wide_mm(jnp.maximum(wide_mm(queries[:slots], hyper_ref[0]), 0.0), hyper_ref[1])
    hyper = hyper.astype(bf16).astype(f32) * gains_ref[3:4]
    hyper = (hyper - jnp.mean(hyper, axis=1, keepdims=True)).astype(bf16)
    apart, middle = moves[: HEADS * slots], moves[HEADS * slots :]
    middle_wide, hyper_wide = middle.astype(f32), hyper.astype(f32)
    consts = jnp.concatenate(
        [
            jnp.sum(middle_wide * middle_wide, axis=1, keepdims=True),
            jnp.sum(middle_wide * hyper_wide, axis=1, keepdims=True),
        ],
        axis=1,
    )
    block = HEADS * SLOT_GROUP
    tall = block + 2 * SLOT_GROUP
    row_slot = lax.rem(lax.broadcasted_iota(jnp.int32, (tall, block), 0), SLOT_GROUP)
    column_slot = lax.rem(lax.broadcasted_iota(jnp.int32, (tall, block), 1), SLOT_GROUP)
    on_weights = []
    for at in range(0, slots, SLOT_GROUP):
        mine = apart[at * HEADS : (at + SLOT_GROUP) * HEADS]
        centre_twice = (2.0 * middle_wide[at : at + SLOT_GROUP]).astype(bf16)
        mask = hyper[at : at + SLOT_GROUP]
        crossed = mm_t(jnp.concatenate([mine, centre_twice, mask], axis=0), mine)
        crossed = jnp.where(row_slot == column_slot, crossed, 0.0).astype(bf16)
        folded = jnp.concatenate(
            [
                twice[at * HEADS : (at + SLOT_GROUP) * HEADS],
                twice[HEADS * slots + at : HEADS * slots + at + SLOT_GROUP],
                jnp.zeros((SLOT_GROUP, inner), bf16),
            ],
            axis=0,
        )
        on_weights.append(jnp.concatenate([folded, crossed], axis=1))
    on_cells = jnp.concatenate([out_centred, hyper], axis=0)
    on_weights = jnp.concatenate(on_weights, axis=0)
    gaps_ref[...] = gaps
    on_cells_ref[...] = on_cells
    on_weights_ref[...] = on_weights
    consts_ref[...] = consts

    live = counts_ref[0, lax.axis_index("row")]
    seam_cells = seam_cells_ref[...].astype(bf16)
    found = cell_weights(gaps, seam_keys_ref[...].astype(bf16), on_cells, seam_cells)
    _, covers = cell_logits(found, seam_cells, on_weights, consts, live)
    count = 2 * SEAM * side
    line = lax.broadcasted_iota(jnp.int32, (side, count), 0)
    column = lax.broadcasted_iota(jnp.int32, (side, count), 1)
    near = (column >= line * 2 * SEAM) & (column < (line + 1) * 2 * SEAM)
    ours = lax.rem(lax.broadcasted_iota(jnp.int32, (count, side), 0), 2 * SEAM)
    theirs = lax.broadcasted_iota(jnp.int32, (count, side), 1)
    left = jnp.where(ours < SEAM, SEAM + 1 - (side + ours - theirs), 0)
    right = jnp.where(ours >= SEAM, SEAM + 1 - (theirs + 2 * SEAM - ours), 0)
    lines = jnp.where(near, covers, 0.0)
    scale = 1.0 / (SEAM + 1) ** 2
    to_left = scale * wide_mm(lines, jnp.maximum(left, 0).astype(f32).astype(bf16))
    to_right = scale * wide_mm(lines, jnp.maximum(right, 0).astype(f32).astype(bf16))
    column = lax.axis_index("col")
    to_left = jnp.where(column > 0, to_left, 0.0)
    to_right = jnp.where(column < lax.axis_size("col") - 1, to_right, 0.0)
    even = lax.rem(column, 2) == 0
    even_ref[...] = jnp.where(even, to_right, to_left)
    odd_ref[...] = jnp.where(even, to_left, to_right)


def image_kernel(
    counts_ref,
    cells_ref,
    keys_ref,
    gaps_ref,
    on_cells_ref,
    on_weights_ref,
    consts_ref,
    logits_ref,
    blended_ref,
    coverage_ref,
    found_ref,
    sems,
):
    pixels, width = cells_ref.shape
    side = math.isqrt(pixels)
    live = counts_ref[0, lax.axis_index("row")]
    gaps, on_cells, on_weights = gaps_ref[...], on_cells_ref[...], on_weights_ref[...]
    consts = consts_ref[...]
    places = [slice(at, at + CELLS_AT_ONCE) for at in range(0, pixels, CELLS_AT_ONCE)]
    copies = []

    def begin(place):
        return cell_weights(gaps, keys_ref[place, :], on_cells, cells_ref[place, :])

    ahead = begin(places[0])
    for step, place in enumerate(places):
        found = ahead
        if step + 1 < len(places):
            ahead = begin(places[step + 1])
        logits, covers = cell_logits(found, cells_ref[place, :], on_weights, consts, live)
        found_ref[:, place] = logits
        copies.append(
            pltpu.make_async_copy(found_ref.at[:, place], logits_ref.at[:, place], sems.at[step])
        )
        copies[-1].start()
        for at in range(0, CELLS_AT_ONCE, side):
            line = (step * CELLS_AT_ONCE + at) // side
            coverage_ref[line : line + 1, :] = covers[:, at : at + side]
    apart = jnp.abs(
        lax.broadcasted_iota(jnp.int32, (side, side), 0)
        - lax.broadcasted_iota(jnp.int32, (side, side), 1)
    )
    band = jnp.maximum(SEAM + 1 - apart, 0).astype(f32).astype(bf16)
    blended_ref[...] = (1.0 / (SEAM + 1) ** 2) * wide_mm(coverage_ref[...], band)
    for copy in copies:
        copy.wait()


def shards(
    embedding,
    counts,
    points,
    pe_gauss,
    point_embed,
    mask_token,
    sa_qkv,
    sa_out,
    t2i_qkv,
    t2i_out,
    mlp_up,
    mlp_down,
    i2t_qkv,
    i2t_out,
    hyper_w,
    ln_gains,
):
    side = embedding.shape[0]
    width = embedding.shape[2]
    inner = t2i_qkv.shape[1] // 3
    slots = points.shape[3]
    pixels = side * side
    groups = slots // SLOT_GROUP
    tall = (HEADS + 2) * SLOT_GROUP
    whole = pl.BlockSpec(memory_space=pltpu.VMEM)
    scalars = pl.BlockSpec(memory_space=pltpu.SMEM)
    cells = embedding.reshape(pixels, width)
    shape = jax.ShapeDtypeStruct
    params = pltpu.CompilerParams(vmem_limit_bytes=36 << 20)
    far = pl.BlockSpec(memory_space=pltpu.HBM)
    arrays = [
        pltpu.with_memory_space_constraint(one, pltpu.HBM)
        for one in (
            counts,
            points.reshape(2, slots),
            pe_gauss,
            point_embed.reshape(1, width),
            mask_token.reshape(1, width),
            sa_qkv,
            sa_out,
            t2i_qkv,
            t2i_out,
            mlp_up,
            mlp_down,
            i2t_qkv,
            i2t_out,
            hyper_w,
            ln_gains,
            cells,
        )
    ]
    *slot_side, even, odd = pl.pallas_call(
        decode_kernel,
        out_shape=(
            shape((pixels, width), bf16),
            shape((pixels, width), bf16),
            shape((HEADS * slots, width), bf16),
            shape((inner + slots, width), bf16),
            shape((groups * tall, inner + HEADS * SLOT_GROUP), bf16),
            shape((slots, 2), f32),
            shape((side, side), f32),
            shape((side, side), f32),
        ),
        in_specs=[far] * ARRAYS,
        out_specs=(whole,) * 8,
        scratch_shapes=[pltpu.SMEM(counts.shape, counts.dtype)]
        + [pltpu.VMEM(one.shape, one.dtype) for one in arrays[1:-1]]
        + [
            pltpu.SemaphoreType.DMA((ARRAYS,)),
            pltpu.VMEM((2 * SEAM * side, width), f32),
            pltpu.VMEM((2 * SEAM * side, width), f32),
            pltpu.VMEM((inner, pixels), bf16),
            pltpu.VMEM((inner, 2 * slots * HEADS), f32),
        ],
        compiler_params=params,
        name="decode",
    )(*arrays)
    count = lax.axis_size("col")
    rows = lax.axis_size("row")
    swaps = []
    for first in (0, 1):
        pairs = []
        for row in range(rows):
            for column in range(count):
                other = column + 1 if column % 2 == first else column - 1
                if 0 <= other < count:
                    partner = row * count + other
                else:
                    partner = min(row ^ 1, rows - 1) * count + column
                pairs.append((row * count + column, partner))
        swaps.append(pairs)
    odd = lax.ppermute(odd, ("row", "col"), swaps[1])
    even = lax.ppermute(even, ("row", "col"), swaps[0])
    logits, blended = pl.pallas_call(
        image_kernel,
        out_shape=(shape((slots, pixels), bf16), shape((side, side), f32)),
        in_specs=[scalars] + [whole] * 6,
        out_specs=(pl.BlockSpec(memory_space=pltpu.HBM), whole),
        scratch_shapes=[
            pltpu.VMEM((side, side), f32),
            pltpu.VMEM((slots, pixels), bf16),
            pltpu.SemaphoreType.DMA((pixels // CELLS_AT_ONCE,)),
        ],
        compiler_params=params,
        name="image",
    )(arrays[0], *slot_side)
    return (logits.reshape(1, 1, slots, pixels), blended + even + odd)


def solution(mesh):
    placed = (P("row", "col", None), P("col", None), P("row", "col", None, None)) + (P(),) * 13
    return jax.shard_map(
        shards,
        mesh=mesh,
        in_specs=placed,
        out_specs=(P("row", "col", None, None), P("row", "col")),
        check_vma=False,
    )
```

```python
import functools
import math

import jax
import jax.numpy as jnp
from jax import lax
from jax.experimental import pallas as pl
from jax.experimental.pallas import tpu as pltpu
from jax.sharding import PartitionSpec as P

HEADS = 8
SEAM = 4
IMG = 1024
SLOT_GROUP = 16
KEYS_AT_ONCE = 1024
PROBES_AT_ONCE = 256
FOLD = 64
IN_RANGE = 2.0**96
ARRAYS = 16
FETCH_ORDER = (2, 1, 4, 3, 14, 5, 6, 7, 15, 8, 9, 10, 11, 12, 13, 0)
CELLS_AT_ONCE = 512

norm_eps = 1e-05
bf16 = jnp.bfloat16
f32 = jnp.float32


def mm(left, right):
    return lax.dot_general(left, right, (((1,), (0,)), ((), ())), preferred_element_type=f32)


def mm_t(left, right):
    return lax.dot_general(left, right, (((1,), (1,)), ((), ())), preferred_element_type=f32)


def halves(values):
    high = values.astype(bf16)
    low = (values - high.astype(f32)).astype(bf16)
    return jnp.concatenate([high, low], axis=0)


def wide_mm(values, weight, product=mm):
    rows = values.shape[0]
    both = product(halves(values), weight)
    return both[:rows] + both[rows:]


def token_mm(values, weight):
    return mm(values.astype(bf16), weight)


def layer_norm(values, gain):
    centred = values - jnp.mean(values, axis=-1, keepdims=True)
    spread = jnp.mean(centred * centred, axis=-1, keepdims=True)
    return centred * lax.rsqrt(spread + norm_eps) * gain


def sin_turns(turns):
    part = turns - jnp.floor(turns + 0.5)
    size = 0.25 - jnp.abs(jnp.abs(part) - 0.25)
    angle = (2.0 * math.pi) * jnp.where(part < 0.0, -size, size)
    square = angle * angle
    total = jnp.full_like(angle, -1.0 / math.factorial(11))
    for order in (9, 7, 5, 3, 1):
        sign = 1.0 if order % 4 == 1 else -1.0
        total = total * square + sign / math.factorial(order)
    return total * angle


def fold_rows(values, join):
    total = values[:FOLD]
    for at in range(FOLD, values.shape[0], FOLD):
        total = join(total, values[at : at + FOLD])
    rows = FOLD
    while rows > 1:
        rows //= 2
        total = join(total[:rows], total[rows:])
    return total


def by_head(rows, inner_width):
    head_width = inner_width // HEADS
    lane = lax.broadcasted_iota(jnp.int32, rows.shape, 1)
    return jnp.concatenate(
        [
            jnp.where((lane >= h * head_width) & (lane < (h + 1) * head_width), rows, 0.0)
            for h in range(HEADS)
        ],
        axis=0,
    )


def by_group(rows, inner_width):
    return jnp.concatenate(
        [
            by_head(rows[at : at + SLOT_GROUP], inner_width)
            for at in range(0, rows.shape[0], SLOT_GROUP)
        ],
        axis=0,
    )


def group_ones(width, group):
    row = lax.broadcasted_iota(jnp.int32, (width, width), 0)
    column = lax.broadcasted_iota(jnp.int32, (width, width), 1)
    first = row - lax.rem(row, group)
    return jnp.where((column >= first) & (column < first + group), 1.0, 0.0).astype(bf16)


def cell_weights(gaps, keys, on_cells, cells):
    slots = gaps.shape[0] // HEADS
    flat = mm_t(on_cells, cells)
    weights = jnp.tanh(mm_t(gaps, keys)).astype(bf16)
    return flat[:-slots].astype(bf16), weights, flat[-slots:]


def cell_logits(found, cells, on_weights, consts, live):
    folds, weights, products = found
    count, width = cells.shape
    slots = consts.shape[0]
    block = HEADS * SLOT_GROUP
    tall = block + 2 * SLOT_GROUP
    wide = cells.astype(f32)
    wide = wide - jnp.mean(wide, axis=1, keepdims=True)
    norms = jnp.sum(wide * wide, axis=1, keepdims=True)
    lanes = 128
    same = lax.broadcasted_iota(jnp.int32, (lanes, lanes), 0) == lax.broadcasted_iota(
        jnp.int32, (lanes, lanes), 1
    )
    norms = jnp.concatenate(
        [
            jnp.sum(jnp.where(same, norms[at : at + lanes], 0.0), axis=0, keepdims=True)
            for at in range(0, count, lanes)
        ],
        axis=1,
    )
    logits, covers = [], []
    for at in range(0, slots, SLOT_GROUP):
        group = at // SLOT_GROUP
        mine = weights[group * block : (group + 1) * block]
        both = mm(
            on_weights[group * tall : (group + 1) * tall], jnp.concatenate([folds, mine], axis=0)
        )
        square = norms + both[block : block + SLOT_GROUP] + consts[at : at + SLOT_GROUP, 0:1]
        for h in range(HEADS):
            part = slice(h * SLOT_GROUP, (h + 1) * SLOT_GROUP)
            square = square + mine[part].astype(f32) * both[part]
        dots = both[block + SLOT_GROUP :] + products[at : at + SLOT_GROUP]
        dots = dots + consts[at : at + SLOT_GROUP, 1:2]
        kept = at + lax.broadcasted_iota(jnp.int32, (SLOT_GROUP, count), 0) < live
        found = dots * lax.rsqrt(jnp.maximum(square, 0.0) + width * norm_eps)
        found = jnp.where(kept, found, 0.0).astype(bf16)
        logits.append(found)
        covers.append(jnp.where(kept, 0.5 * jnp.tanh(0.5 * found.astype(f32)) + 0.5, 0.0))
    return jnp.concatenate(logits, axis=0), jnp.sum(sum(covers), axis=0, keepdims=True)


def decode_kernel(*refs):
    far, refs = refs[:ARRAYS], refs[ARRAYS:]
    (cells_ref, *slot_side), refs = refs[:8], refs[8:]
    near, (sems, *scratch) = refs[: ARRAYS - 1], refs[ARRAYS - 1 :]
    near = [*near, cells_ref]
    copies = [pltpu.make_async_copy(*pair, sems.at[at]) for at, pair in enumerate(zip(far, near))]
    for at in FETCH_ORDER:
        copies[at].start()
    decode(copies, *near, *slot_side, *scratch)


def decode(
    copies,
    counts_ref,
    points_ref,
    gauss_ref,
    point_embed_ref,
    mask_token_ref,
    sa_qkv_ref,
    sa_out_ref,
    t2i_qkv_ref,
    t2i_out_ref,
    mlp_up_ref,
    mlp_down_ref,
    i2t_qkv_ref,
    i2t_out_ref,
    hyper_ref,
    gains_ref,
    cells_ref,
    keys_ref,
    gaps_ref,
    on_cells_ref,
    on_weights_ref,
    consts_ref,
    even_ref,
    odd_ref,
    seam_cells_ref,
    seam_keys_ref,
    values_ref,
    pooled_ref,
):
    pixels, width = cells_ref.shape
    side = math.isqrt(pixels)
    slots = points_ref.shape[1]
    inner = t2i_qkv_ref.shape[1] // 3
    head_width = inner // HEADS
    half = width // 2
    for at in FETCH_ORDER[:5]:
        copies[at].wait()

    gauss = gauss_ref[...]
    steps = lax.broadcasted_iota(jnp.int32, (side, half), 0).astype(f32)
    steps = (2.0 * (steps + 0.5)) / side - 1.0
    spots = jnp.clip(points_ref[...], 0, IMG - 1).astype(f32)
    spots = 2.0 * ((spots + 0.5) / IMG) - 1.0
    same = lax.broadcasted_iota(jnp.int32, (slots, slots), 0) == lax.broadcasted_iota(
        jnp.int32, (slots, slots), 1
    )
    spot_x = jnp.sum(jnp.where(same, spots[0:1], 0.0), axis=1, keepdims=True)
    spot_y = jnp.sum(jnp.where(same, spots[1:2], 0.0), axis=1, keepdims=True)
    turns = jnp.concatenate(
        [steps * gauss[0:1], steps * gauss[1:2], spot_x * gauss[0:1] + spot_y * gauss[1:2]], axis=0
    )
    sines = sin_turns(turns)
    cosines = sin_turns(turns + 0.25)
    prompt = jnp.concatenate([sines[2 * side :], cosines[2 * side :]], axis=1)

    start = jnp.concatenate(
        [
            jnp.broadcast_to(mask_token_ref[...], (slots, width)),
            prompt + point_embed_ref[...],
        ],
        axis=0,
    )
    for at in FETCH_ORDER[5:8]:
        copies[at].wait()
    qkv = wide_mm(start, sa_qkv_ref[...])
    query, key, value = qkv[:, :width], qkv[:, width : 2 * width], qkv[:, 2 * width :]
    key_gap = key[:slots] - key[slots:]
    value_gap = value[:slots] - value[slots:]
    scores = wide_mm(
        query * jnp.concatenate([key_gap, key_gap], axis=0), group_ones(width, width // HEADS)
    )
    first = 0.5 * jnp.tanh((0.5 / math.sqrt(width // HEADS)) * scores) + 0.5
    attended = jnp.concatenate([value[slots:]] * 2, axis=0) + first * jnp.concatenate(
        [value_gap, value_gap], axis=0
    )
    queries = layer_norm(wide_mm(attended, sa_out_ref[...]), gains_ref[0:1])
    head_scale = 1.0 / math.sqrt(head_width)
    cross_q = wide_mm(queries + start, t2i_qkv_ref[:, :inner])
    cross_q = by_head(cross_q, inner).astype(bf16)
    probes = mm_t(cross_q, t2i_qkv_ref[:, inner : 2 * inner]) * (head_scale * math.log2(math.e))
    probes = probes.astype(bf16)

    copies[FETCH_ORDER[8]].wait()
    sin_x, cos_x = sines[:side], cosines[:side]
    left_half = lax.broadcasted_iota(jnp.int32, (2 * SEAM, width), 0) < SEAM
    for line in range(side):
        sin_y, cos_y = sines[side + line : side + line + 1], cosines[side + line : side + line + 1]
        place = slice(line * side, (line + 1) * side)
        encoding = jnp.concatenate(
            [sin_x * cos_y + cos_x * sin_y, cos_x * cos_y - sin_x * sin_y], axis=1
        )
        own = cells_ref[place, :].astype(f32)
        keys = own + encoding
        keys_ref[place, :] = keys.astype(bf16)
        seam = slice(line * 2 * SEAM, (line + 1) * 2 * SEAM)
        seam_cells_ref[seam, :] = jnp.where(left_half, own[: 2 * SEAM], own[side - 2 * SEAM :])
        seam_keys_ref[seam, :] = jnp.where(left_half, keys[: 2 * SEAM], keys[side - 2 * SEAM :])

    values_ref[...] = mm_t(
        t2i_qkv_ref[:, 2 * inner :].astype(f32).T.astype(bf16), cells_ref[...]
    ).astype(bf16)
    tokens = start.shape[0]
    ones = jnp.ones((head_width, KEYS_AT_ONCE), bf16)
    tiles = []
    for at in range(0, HEADS * tokens, PROBES_AT_ONCE):
        rows = slice(
            at // tokens * head_width, ((at + PROBES_AT_ONCE - 1) // tokens + 1) * head_width
        )
        tiles.append((rows, slice(at, at + PROBES_AT_ONCE)))

    def raw_scores(cell):
        return mm_t(keys_ref[cell : cell + KEYS_AT_ONCE, :], probes)

    def pool(cell, rows, share):
        near = values_ref[rows, cell : cell + KEYS_AT_ONCE]
        return mm(jnp.concatenate([near, ones], axis=0), share)

    sums = [0.0] * len(tiles)
    ahead = raw_scores(0)
    for cell in range(0, pixels, KEYS_AT_ONCE):
        raw = ahead
        if cell + KEYS_AT_ONCE < pixels:
            ahead = raw_scores(cell + KEYS_AT_ONCE)
        share = jnp.exp2(raw).astype(bf16)
        sums = [
            total + pool(cell, rows, share[:, lanes]) for total, (rows, lanes) in zip(sums, tiles)
        ]
    inside = []
    for total, (rows, lanes) in zip(sums, tiles):
        whole = total[-head_width : -head_width + 1]
        inside.append((whole >= 1.0 / IN_RANGE) & (whole <= IN_RANGE))
        pooled_ref[rows, lanes] = total[:-head_width] / whole
    inside = jnp.min(jnp.concatenate(inside, axis=1).astype(f32))

    @pl.when(inside < 0.5)
    def _():
        sums = [0.0] * len(tiles)
        for cell in range(0, pixels, KEYS_AT_ONCE):
            raw = raw_scores(cell)
            top = fold_rows(raw, jnp.maximum)
            if cell > 0:
                top = jnp.maximum(top, old_top)
                fade = jnp.exp2(old_top - top)
                sums = [total * fade[:, lanes] for total, (rows, lanes) in zip(sums, tiles)]
            old_top = top
            share = jnp.exp2(raw - top).astype(bf16)
            sums = [
                total + pool(cell, rows, share[:, lanes])
                for total, (rows, lanes) in zip(sums, tiles)
            ]
        for total, (rows, lanes) in zip(sums, tiles):
            pooled_ref[rows, lanes] = total[:-head_width] / total[-head_width : -head_width + 1]

    joined = jnp.concatenate(
        [
            pooled_ref[h * head_width : (h + 1) * head_width, h * tokens : (h + 1) * tokens]
            for h in range(HEADS)
        ],
        axis=0,
    ).T
    for at in FETCH_ORDER[9:]:
        copies[at].wait()
    queries = layer_norm(queries + wide_mm(joined, t2i_out_ref[...]), gains_ref[1:2])
    hidden = jnp.maximum(token_mm(queries, mlp_up_ref[...]), 0.0)
    queries = layer_norm(queries + token_mm(hidden, mlp_down_ref[...]), gains_ref[2:3])

    back_k = wide_mm(queries + start, i2t_qkv_ref[:, inner : 2 * inner])
    back_v = wide_mm(queries, i2t_qkv_ref[:, 2 * inner :])
    gaps = by_group(back_k[:slots] - back_k[slots:], inner)
    gaps = mm_t(gaps.astype(bf16), i2t_qkv_ref[:, :inner]) * (0.5 * head_scale)
    gaps = gaps.astype(bf16)
    middle = 0.5 * (back_v[:slots] + back_v[slots:])
    apart = by_group(0.5 * (back_v[:slots] - back_v[slots:]), inner)
    twice = (2.0 * jnp.concatenate([apart, middle], axis=0)).astype(bf16)
    out_wide = i2t_out_ref[...].astype(f32)
    out_centred = (out_wide - jnp.mean(out_wide, axis=1, keepdims=True)).astype(bf16)
    moves = 0.5 * mm(twice, i2t_out_ref[...])
    moves = (moves - jnp.mean(moves, axis=1, keepdims=True)).astype(bf16)
    hyper = wide_mm(jnp.maximum(wide_mm(queries[:slots], hyper_ref[0]), 0.0), hyper_ref[1])
    hyper = hyper.astype(bf16).astype(f32) * gains_ref[3:4]
    hyper = (hyper - jnp.mean(hyper, axis=1, keepdims=True)).astype(bf16)
    apart, middle = moves[: HEADS * slots], moves[HEADS * slots :]
    middle_wide, hyper_wide = middle.astype(f32), hyper.astype(f32)
    consts = jnp.concatenate(
        [
            jnp.sum(middle_wide * middle_wide, axis=1, keepdims=True),
            jnp.sum(middle_wide * hyper_wide, axis=1, keepdims=True),
        ],
        axis=1,
    )
    block = HEADS * SLOT_GROUP
    tall = block + 2 * SLOT_GROUP
    row_slot = lax.rem(lax.broadcasted_iota(jnp.int32, (tall, block), 0), SLOT_GROUP)
    column_slot = lax.rem(lax.broadcasted_iota(jnp.int32, (tall, block), 1), SLOT_GROUP)
    on_weights = []
    for at in range(0, slots, SLOT_GROUP):
        mine = apart[at * HEADS : (at + SLOT_GROUP) * HEADS]
        centre_twice = (2.0 * middle_wide[at : at + SLOT_GROUP]).astype(bf16)
        mask = hyper[at : at + SLOT_GROUP]
        crossed = mm_t(jnp.concatenate([mine, centre_twice, mask], axis=0), mine)
        crossed = jnp.where(row_slot == column_slot, crossed, 0.0).astype(bf16)
        folded = jnp.concatenate(
            [
                twice[at * HEADS : (at + SLOT_GROUP) * HEADS],
                twice[HEADS * slots + at : HEADS * slots + at + SLOT_GROUP],
                jnp.zeros((SLOT_GROUP, inner), bf16),
            ],
            axis=0,
        )
        on_weights.append(jnp.concatenate([folded, crossed], axis=1))
    on_cells = jnp.concatenate([out_centred, hyper], axis=0)
    on_weights = jnp.concatenate(on_weights, axis=0)
    gaps_ref[...] = gaps
    on_cells_ref[...] = on_cells
    on_weights_ref[...] = on_weights
    consts_ref[...] = consts

    live = counts_ref[0, lax.axis_index("row")]
    seam_cells = seam_cells_ref[...].astype(bf16)
    found = cell_weights(gaps, seam_keys_ref[...].astype(bf16), on_cells, seam_cells)
    _, covers = cell_logits(found, seam_cells, on_weights, consts, live)
    count = 2 * SEAM * side
    line = lax.broadcasted_iota(jnp.int32, (side, count), 0)
    column = lax.broadcasted_iota(jnp.int32, (side, count), 1)
    near = (column >= line * 2 * SEAM) & (column < (line + 1) * 2 * SEAM)
    ours = lax.rem(lax.broadcasted_iota(jnp.int32, (count, side), 0), 2 * SEAM)
    theirs = lax.broadcasted_iota(jnp.int32, (count, side), 1)
    left = jnp.where(ours < SEAM, SEAM + 1 - (side + ours - theirs), 0)
    right = jnp.where(ours >= SEAM, SEAM + 1 - (theirs + 2 * SEAM - ours), 0)
    lines = jnp.where(near, covers, 0.0)
    scale = 1.0 / (SEAM + 1) ** 2
    to_left = scale * wide_mm(lines, jnp.maximum(left, 0).astype(f32).astype(bf16))
    to_right = scale * wide_mm(lines, jnp.maximum(right, 0).astype(f32).astype(bf16))
    column = lax.axis_index("col")
    to_left = jnp.where(column > 0, to_left, 0.0)
    to_right = jnp.where(column < lax.axis_size("col") - 1, to_right, 0.0)
    even = lax.rem(column, 2) == 0
    even_ref[...] = jnp.where(even, to_right, to_left)
    odd_ref[...] = jnp.where(even, to_left, to_right)


def image_kernel(
    counts_ref,
    cells_ref,
    keys_ref,
    gaps_ref,
    on_cells_ref,
    on_weights_ref,
    consts_ref,
    logits_ref,
    blended_ref,
    coverage_ref,
    found_ref,
    sems,
):
    pixels, width = cells_ref.shape
    side = math.isqrt(pixels)
    live = counts_ref[0, lax.axis_index("row")]
    gaps, on_cells, on_weights = gaps_ref[...], on_cells_ref[...], on_weights_ref[...]
    consts = consts_ref[...]
    places = [slice(at, at + CELLS_AT_ONCE) for at in range(0, pixels, CELLS_AT_ONCE)]
    copies = []

    def begin(place):
        return cell_weights(gaps, keys_ref[place, :], on_cells, cells_ref[place, :])

    ahead = begin(places[0])
    for step, place in enumerate(places):
        found = ahead
        if step + 1 < len(places):
            ahead = begin(places[step + 1])
        logits, covers = cell_logits(found, cells_ref[place, :], on_weights, consts, live)
        found_ref[:, place] = logits
        copies.append(
            pltpu.make_async_copy(found_ref.at[:, place], logits_ref.at[:, place], sems.at[step])
        )
        copies[-1].start()
        for at in range(0, CELLS_AT_ONCE, side):
            line = (step * CELLS_AT_ONCE + at) // side
            coverage_ref[line : line + 1, :] = covers[:, at : at + side]
    apart = jnp.abs(
        lax.broadcasted_iota(jnp.int32, (side, side), 0)
        - lax.broadcasted_iota(jnp.int32, (side, side), 1)
    )
    band = jnp.maximum(SEAM + 1 - apart, 0).astype(f32).astype(bf16)
    blended_ref[...] = (1.0 / (SEAM + 1) ** 2) * wide_mm(coverage_ref[...], band)
    for copy in copies:
        copy.wait()


def shards(
    embedding,
    counts,
    points,
    pe_gauss,
    point_embed,
    mask_token,
    sa_qkv,
    sa_out,
    t2i_qkv,
    t2i_out,
    mlp_up,
    mlp_down,
    i2t_qkv,
    i2t_out,
    hyper_w,
    ln_gains,
):
    side = embedding.shape[0]
    width = embedding.shape[2]
    inner = t2i_qkv.shape[1] // 3
    slots = points.shape[3]
    pixels = side * side
    groups = slots // SLOT_GROUP
    tall = (HEADS + 2) * SLOT_GROUP
    whole = pl.BlockSpec(memory_space=pltpu.VMEM)
    scalars = pl.BlockSpec(memory_space=pltpu.SMEM)
    cells = embedding.reshape(pixels, width)
    shape = jax.ShapeDtypeStruct
    params = pltpu.CompilerParams(vmem_limit_bytes=36 << 20)
    far = pl.BlockSpec(memory_space=pltpu.HBM)
    arrays = [
        pltpu.with_memory_space_constraint(one, pltpu.HBM)
        for one in (
            counts,
            points.reshape(2, slots),
            pe_gauss,
            point_embed.reshape(1, width),
            mask_token.reshape(1, width),
            sa_qkv,
            sa_out,
            t2i_qkv,
            t2i_out,
            mlp_up,
            mlp_down,
            i2t_qkv,
            i2t_out,
            hyper_w,
            ln_gains,
            cells,
        )
    ]
    *slot_side, even, odd = pl.pallas_call(
        decode_kernel,
        out_shape=(
            shape((pixels, width), bf16),
            shape((pixels, width), bf16),
            shape((HEADS * slots, width), bf16),
            shape((inner + slots, width), bf16),
            shape((groups * tall, inner + HEADS * SLOT_GROUP), bf16),
            shape((slots, 2), f32),
            shape((side, side), f32),
            shape((side, side), f32),
        ),
        in_specs=[far] * ARRAYS,
        out_specs=(whole,) * 8,
        scratch_shapes=[pltpu.SMEM(counts.shape, counts.dtype)]
        + [pltpu.VMEM(one.shape, one.dtype) for one in arrays[1:-1]]
        + [
            pltpu.SemaphoreType.DMA((ARRAYS,)),
            pltpu.VMEM((2 * SEAM * side, width), f32),
            pltpu.VMEM((2 * SEAM * side, width), f32),
            pltpu.VMEM((inner, pixels), bf16),
            pltpu.VMEM((inner, 2 * slots * HEADS), f32),
        ],
        compiler_params=params,
        name="decode",
    )(*arrays)
    count = lax.axis_size("col")
    rows = lax.axis_size("row")
    swaps = []
    for first in (0, 1):
        pairs = []
        for row in range(rows):
            for column in range(count):
                other = column + 1 if column % 2 == first else column - 1
                if 0 <= other < count:
                    partner = row * count + other
                else:
                    partner = min(row ^ 1, rows - 1) * count + column
                pairs.append((row * count + column, partner))
        swaps.append(pairs)
    odd = lax.ppermute(odd, ("row", "col"), swaps[1])
    even = lax.ppermute(even, ("row", "col"), swaps[0])
    logits, blended = pl.pallas_call(
        image_kernel,
        out_shape=(shape((slots, pixels), bf16), shape((side, side), f32)),
        in_specs=[scalars] + [whole] * 6,
        out_specs=(pl.BlockSpec(memory_space=pltpu.HBM), whole),
        scratch_shapes=[
            pltpu.VMEM((side, side), f32),
            pltpu.VMEM((slots, pixels), bf16),
            pltpu.SemaphoreType.DMA((pixels // CELLS_AT_ONCE,)),
        ],
        compiler_params=params,
        name="image",
    )(arrays[0], *slot_side)
    return (logits.reshape(1, 1, slots, pixels), blended + even + odd)


def solution(mesh):
    placed = (P("row", "col", None), P("col", None), P("row", "col", None, None)) + (P(),) * 13
    return jax.shard_map(
        shards,
        mesh=mesh,
        in_specs=placed,
        out_specs=(P("row", "col", None, None), P("row", "col")),
        check_vma=False,
    )
```
